128 devices in a mesh: member: 8 (over y_lo, z), dp: 16 (over y_hi, x, core).
Axes of the slice: x: 4, y: 4 (y_hi: 2, y_lo: 2; y = y_hi * 2 + y_lo), z: 4, core: 2. Of those that a mesh axis runs over, the one named last changes fastest.
Arguments:
- hidden: bfloat16 [8, 8192, 4096], P('member', 'dp'), may hold values from -8 to 8
- projection: bfloat16 [8, 4096, 1024], P('member', 'dp'), may hold values from -0.09375 to 0.09375
- head_weight: bfloat16 [8, 14, 1024], P('member'), may hold values from -0.375 to 0.375
- head_bias: float32 [8, 14], P('member'), may hold values from -4 to 4
- prior_precision: float32 [8, 1024], P('member'), may hold values from 0.5 to 5
- labels: int32 [8192], P('dp'), may hold values from 0 to 13
- category_weight: int32 [14], replicated, may hold values from 1 to 9
Outputs:
- variance: float32 [8, 8192], P('member', 'dp')
- ensemble_probs: float32 [14, 8192], P(None, 'dp')
The draws below stay inside these ranges and needn't reach their ends.
All inputs are finite; a program needn't handle non-finite values.
Results may differ from the reference program's by a relative error of at most 0.0025.
Values may be sent and summed in bfloat16 or wider, within the bound.
A program may use at most 128 MiB of HBM per device.

```python
import math
import jax
import jax.numpy as jnp
from jax import lax

D = 4096
P_SIZE = 1024
C = 14
MEMBERS = 8
ROWS = 8192


def draw_hidden(key, part):
    first, second, third, fourth = jax.random.split(key, 4)
    noise = jax.random.normal(first, (MEMBERS, ROWS, D), jnp.float32)
    common = jax.random.normal(second, (MEMBERS, 1, D), jnp.float32)
    amount = 0.8 * jax.random.normal(third, (MEMBERS, ROWS, 1), jnp.float32)
    scales = jnp.exp(jax.random.uniform(fourth, (MEMBERS, 1, D), jnp.float32, -1.2, 1.1))
    values = scales * (noise + amount * common)
    return jnp.clip(values, -8.0, 8.0).astype(jnp.bfloat16)


def set_ends(array, stream_key, smallest, largest):
    place = [jax.random.randint(jax.random.fold_in(stream_key, axis), (), 0, length) for axis, length in enumerate(array.shape)]
    longest = array.shape.index(max(array.shape))
    beside = place[:longest] + [(place[longest] + 1) % array.shape[longest]] + place[longest + 1:]
    return array.at[tuple(place)].set(smallest).at[tuple(beside)].set(largest)


def level_of(own_key, shape, pieces, smallest, top_value):
    gain, own = 1.0, jax.random.fold_in(own_key, 6)
    for axis_at, parts in pieces:
        steps = jnp.exp(jax.random.uniform(jax.random.fold_in(own, axis_at), (parts,), jnp.float32, smallest / len(pieces), top_value / len(pieces)))
        gain = gain * jnp.repeat(steps, shape[axis_at] // parts).reshape([-1 if axis == axis_at else 1 for axis in range(len(shape))])
    return gain


def normal_values(stream_key, extent, spread, limit, cuts=(), kind=jnp.bfloat16):
    gain = level_of(stream_key, extent, cuts, -0.22, 0.18) if cuts else 1.0
    array = jax.random.normal(stream_key, extent, jnp.float32) * spread * gain
    return jnp.minimum(jnp.maximum(array, -limit), limit).astype(kind)


def setup_inputs(seed: int = 0) -> dict:
    arg_keys = jax.random.split(jax.random.key(seed), 8)
    return {
        "hidden": draw_hidden(jax.random.fold_in(arg_keys[7], 71), 0),
        "projection": normal_values(arg_keys[1], (MEMBERS, D, P_SIZE), D ** -0.5, 0.09375, ((0, 8), (1, 16))),
        "head_weight": normal_values(arg_keys[2], (MEMBERS, C, P_SIZE), (P_SIZE // 4) ** -0.5, 0.375, ((0, 8),)),
        "head_bias": normal_values(arg_keys[3], (MEMBERS, C), 1.0, 4.0, ((0, 8),), jnp.float32),
        "prior_precision": jnp.clip(jnp.exp(math.log(5.0) - 2.3025851 * jax.random.uniform(arg_keys[4], (MEMBERS, P_SIZE), jnp.float32) ** level_of(arg_keys[4], (MEMBERS, P_SIZE), ((0, 8),), -0.2, 0.2)), 0.5, 5.0),
        "labels": set_ends(jax.random.randint(arg_keys[5], (ROWS,), 0, C), jax.random.fold_in(arg_keys[5], 1), 0, C - 1).astype(jnp.int32),
        "category_weight": set_ends(jax.random.randint(arg_keys[6], (C,), 1, 10), jax.random.fold_in(arg_keys[6], 1), 1, 9).astype(jnp.int32),
    }


def reference(hidden, projection, head_weight, head_bias, prior_precision, labels, category_weight):
    onehot = labels[None, :] == jnp.arange(C, dtype=jnp.int32)[:, None]
    row_weight = lax.optimization_barrier(jnp.sum(jnp.where(onehot, category_weight.astype(jnp.float32)[:, None], jnp.float32(0.0)), axis=0))
    variances = []
    total = jnp.zeros((C, ROWS), jnp.float32)
    for member_index in range(MEMBERS):
        features = jnp.dot(hidden[member_index].astype(jnp.float32), projection[member_index].astype(jnp.float32), preferred_element_type=jnp.float32).astype(jnp.bfloat16)
        logits = jnp.dot(head_weight[member_index].astype(jnp.float32), features.T.astype(jnp.float32), preferred_element_type=jnp.float32) + head_bias[member_index][:, None]
        expo = jnp.exp(logits)
        probs = expo / lax.optimization_barrier(jnp.sum(expo, axis=0, keepdims=True))
        curvature = row_weight * (1.0 - lax.optimization_barrier(jnp.sum(probs * probs, axis=0)))
        weighted = (features.astype(jnp.float32) * jnp.sqrt(curvature)[:, None]).astype(jnp.bfloat16)
        gram = jnp.dot(weighted.T.astype(jnp.float32), weighted.astype(jnp.float32), preferred_element_type=jnp.float32)
        precision = gram / ROWS + jnp.diag(prior_precision[member_index])
        factor = jnp.linalg.cholesky(precision)
        solved = lax.linalg.triangular_solve(factor, features.T.astype(jnp.float32), left_side=True, lower=True)
        variance = 4.0 / P_SIZE * lax.optimization_barrier(jnp.sum(solved * solved, axis=0))
        scaled = logits / jnp.sqrt(1.0 + variance)[None, :]
        moder = jnp.exp(scaled)
        moder = moder / lax.optimization_barrier(jnp.sum(moder, axis=0, keepdims=True))
        total = total + moder
        variances.append(variance)
    return (jnp.stack(variances, axis=0), total / MEMBERS)
```

```python
import jax, jax.numpy as jnp
from jax import lax
from jax.experimental import pallas as pl
from jax.experimental.pallas import tpu as pltpu
from jax.sharding import PartitionSpec as P

N = 1024
ROWS = 8192
B = 128
NB = N // B
R_ = 512
W = N + R_
f32 = jnp.float32
bf16 = jnp.bfloat16


def split3(x):
    hi = x.astype(bf16)
    lo = (x - hi.astype(f32)).astype(bf16)
    return hi, lo


def diag_inverse(S):
    G = 8
    n = B // G
    R = list(S)
    lane = lax.broadcasted_iota(jnp.int32, (G, B), 1)
    sub = lax.broadcasted_iota(jnp.int32, (G, B), 0)
    Q = [jnp.where(lane == sub + G * i, f32(1), f32(0)) for i in range(n)]
    out = [None] * n
    for b in range(n):
        c = [[jnp.broadcast_to(R[i][:, G * b + k:G * b + k + 1], (G, B)) for k in range(G)] for i in range(b, n)]
        cb = c[0]
        rb, qb = R[b], Q[b]
        dv = jnp.ones((G, B), f32)
        inv, rj, qj, cs = [], [], [], []
        for j in range(G):
            p = jnp.broadcast_to(cb[j][j:j + 1, :], (G, B))
            iv = 1.0 / p
            dv = jnp.where(sub == j, p, dv)
            m = jnp.where(sub > j, cb[j] * iv, f32(0))
            row = [None] * G
            for k in range(j + 1, G):
                row[k] = jnp.broadcast_to(cb[k][j:j + 1, :], (G, B))
                cb[k] = cb[k] - m * row[k]
            r = jnp.broadcast_to(rb[j:j + 1, :], (G, B))
            q = jnp.broadcast_to(qb[j:j + 1, :], (G, B))
            if j < G - 1:
                rb = rb - m * r
                qb = qb - m * q
            inv.append(iv); rj.append(r); qj.append(q); cs.append(row)
        out[b] = qb * lax.rsqrt(dv)
        for i in range(b + 1, n):
            ci = c[i - b]
            ri, qi = R[i], Q[i]
            for j in range(G):
                m = ci[j] * inv[j]
                for k in range(j + 1, G):
                    ci[k] = ci[k] - m * cs[j][k]
                ri = ri - m * rj[j]
                qi = qi - m * qj[j]
            R[i], Q[i] = ri, qi
    return out


def chol_kernel(a_ref, prior_ref, ft_ref, var_ref, g_ref, linv_ref, ul_ref, ur_ref):
    eye_r = lax.broadcasted_iota(jnp.int32, (B, N), 0)
    eye_c = lax.broadcasted_iota(jnp.int32, (B, N), 1)
    for i in range(NB):
        rows = pl.ds(B * i, B)
        g_ref[rows, :N] = a_ref[rows, :] * f32(1.0 / ROWS) + jnp.where(eye_c == eye_r + B * i, prior_ref[...], f32(0))
        g_ref[rows, N:] = ft_ref[rows, :].astype(f32)
    var_ref[...] = jnp.zeros_like(var_ref)

    @pl.loop(0, NB)
    def _(k):
        k0 = pl.multiple_of(k * B, B)
        S = [g_ref[pl.ds(k0 + 8 * i, 8), pl.ds(k0, B)] for i in range(16)]
        out = diag_inverse(S)
        for i in range(16):
            linv_ref[pl.ds(8 * i, 8), :] = out[i]
        li = linv_ref[...]
        lh, ll = split3(li)
        lcat = jnp.concatenate([lh, ll, lh], axis=1)
        CW = 512
        for c in range(W // CW):
            gh, gl = split3(g_ref[pl.ds(k0, B), CW * c:CW * (c + 1)])
            u = jnp.dot(lcat, jnp.concatenate([gh, gh, gl], axis=0), preferred_element_type=f32)
            uh, ul = split3(u)
            ur_ref[0:B, CW * c:CW * (c + 1)] = uh
            ur_ref[B:2 * B, CW * c:CW * (c + 1)] = uh
            ur_ref[2 * B:, CW * c:CW * (c + 1)] = ul
            if c < N // CW:
                for t in range(CW // B):
                    ut = u[:, B * t:B * (t + 1)].T
                    th, tl = split3(ut)
                    r0 = CW * c + B * t
                    ul_ref[r0:r0 + B, 0:B] = th
                    ul_ref[r0:r0 + B, B:2 * B] = tl
                    ul_ref[r0:r0 + B, 2 * B:] = th
            else:
                var_ref[...] += jnp.sum(u * u, axis=0, keepdims=True)

        @pl.loop(k + 1, NB)
        def _(i):
            i0 = pl.multiple_of(i * B, B)
            lhs = ul_ref[pl.ds(i0, B), :]
            for c in range(W // CW):
                d = jnp.dot(lhs, ur_ref[:, CW * c:CW * (c + 1)], preferred_element_type=f32)
                g_ref[pl.ds(i0, B), CW * c:CW * (c + 1)] -= d
    var_ref[...] = var_ref[...] * (4.0 / N)


def chol_var(a, prior, ft):
    return pl.pallas_call(
        chol_kernel,
        out_shape=jax.ShapeDtypeStruct((1, R_), f32),
        in_specs=[pl.BlockSpec(memory_space=pltpu.VMEM)] * 3,
        out_specs=pl.BlockSpec(memory_space=pltpu.VMEM),
        scratch_shapes=[
            pltpu.VMEM((N, W), f32),
            pltpu.VMEM((B, B), f32),
            pltpu.VMEM((N, 3 * B), bf16),
            pltpu.VMEM((3 * B, W), bf16),
        ],
        compiler_params=pltpu.CompilerParams(vmem_limit_bytes=48 * 1024 * 1024),
    )(a, prior, ft)


def body(hidden, projection, head_weight, head_bias, prior_precision, labels, category_weight):
    local_rows = hidden[0]
    weight_rows = projection[0]
    categories = head_weight.shape[1]
    projected = jnp.dot(
        local_rows,
        lax.all_gather(weight_rows, "dp", axis=0, tiled=True),
        preferred_element_type=f32,
    )
    features = projected.astype(bf16)
    logits = (
        lax.dot_general(head_weight[0], features, (((1,), (1,)), ((), ())), preferred_element_type=f32)
        + head_bias[0][:, None]
    )
    onehot = labels[None, :] == jnp.arange(categories, dtype=jnp.int32)[:, None]
    row_weight = jnp.sum(jnp.where(onehot, category_weight.astype(f32)[:, None], f32(0.0)), axis=0)
    expo = jnp.exp(logits)
    probs = expo / jnp.sum(expo, axis=0, keepdims=True)
    curvature = row_weight * (1.0 - jnp.sum(probs * probs, axis=0))
    weighted = (features * jnp.sqrt(curvature)[:, None]).astype(bf16)
    gram_part = lax.dot_general(weighted, weighted, (((0,), (0,)), ((), ())), preferred_element_type=f32)
    gram = lax.psum(gram_part, "dp")
    variance = chol_var(gram, prior_precision, features.T)[0]
    scaled = logits / jnp.sqrt(1.0 + variance)[None, :]
    moder = jnp.exp(scaled)
    moder = moder / jnp.sum(moder, axis=0, keepdims=True)
    summed = lax.psum(moder, "member")
    ensemble = summed / lax.axis_size("member")
    return (variance[None, :], ensemble)


def solution(mesh):
    return jax.shard_map(
        body,
        mesh=mesh,
        in_specs=(
            P("member", "dp", None),
            P("member", "dp", None),
            P("member", None, None),
            P("member", None),
            P("member", None),
            P("dp"),
            P(),
        ),
        out_specs=(P("member", "dp"), P(None, "dp")),
        check_vma=False,
    )
```

```python
import jax, jax.numpy as jnp
from jax import lax
from jax.experimental import pallas as pl
from jax.experimental.pallas import tpu as pltpu
from jax.sharding import PartitionSpec as P

N = 1024
P_SIZE = 1024
ROWS = 8192
B = 128
NB = N // B
R_ = 512
W = N + R_
f32 = jnp.float32
bf16 = jnp.bfloat16


def split3(x):
    hi = x.astype(bf16)
    lo = (x - hi.astype(f32)).astype(bf16)
    return hi, lo


def diag_inverse(S):
    G = 8
    n = B // G
    R = list(S)
    lane = lax.broadcasted_iota(jnp.int32, (G, B), 1)
    sub = lax.broadcasted_iota(jnp.int32, (G, B), 0)
    Q = [jnp.where(lane == sub + G * i, f32(1), f32(0)) for i in range(n)]
    out = [None] * n
    for b in range(n):
        c = [[jnp.broadcast_to(R[i][:, G * b + k:G * b + k + 1], (G, B)) for k in range(G)] for i in range(b, n)]
        cb = c[0]
        rb, qb = R[b], Q[b]
        dv = jnp.ones((G, B), f32)
        inv, rj, qj, cs = [], [], [], []
        for j in range(G):
            p = jnp.broadcast_to(cb[j][j:j + 1, :], (G, B))
            iv = 1.0 / p
            dv = jnp.where(sub == j, p, dv)
            m = jnp.where(sub > j, cb[j] * iv, f32(0))
            row = [None] * G
            for k in range(j + 1, G):
                row[k] = jnp.broadcast_to(cb[k][j:j + 1, :], (G, B))
                cb[k] = cb[k] - m * row[k]
            r = jnp.broadcast_to(rb[j:j + 1, :], (G, B))
            q = jnp.broadcast_to(qb[j:j + 1, :], (G, B))
            if j < G - 1:
                rb = rb - m * r
                qb = qb - m * q
            inv.append(iv); rj.append(r); qj.append(q); cs.append(row)
        out[b] = qb * lax.rsqrt(dv)
        for i in range(b + 1, n):
            ci = c[i - b]
            ri, qi = R[i], Q[i]
            for j in range(G):
                m = ci[j] * inv[j]
                for k in range(j + 1, G):
                    ci[k] = ci[k] - m * cs[j][k]
                ri = ri - m * rj[j]
                qi = qi - m * qj[j]
            R[i], Q[i] = ri, qi
    return out


def chol_kernel(a_ref, prior_ref, ft_ref, var_ref, g_ref, linv_ref, ul_ref, ur_ref):
    eye_r = lax.broadcasted_iota(jnp.int32, (B, N), 0)
    eye_c = lax.broadcasted_iota(jnp.int32, (B, N), 1)
    for i in range(NB):
        rows = pl.ds(B * i, B)
        g_ref[rows, :N] = a_ref[rows, :] * f32(1.0 / ROWS) + jnp.where(eye_c == eye_r + B * i, prior_ref[...], f32(0))
        g_ref[rows, N:] = ft_ref[rows, :].astype(f32)
    var_ref[...] = jnp.zeros_like(var_ref)

    @pl.loop(0, NB)
    def _(k):
        k0 = pl.multiple_of(k * B, B)
        S = [g_ref[pl.ds(k0 + 8 * i, 8), pl.ds(k0, B)] for i in range(16)]
        out = diag_inverse(S)
        for i in range(16):
            linv_ref[pl.ds(8 * i, 8), :] = out[i]
        li = linv_ref[...]
        lh, ll = split3(li)
        lcat = jnp.concatenate([lh, ll, lh], axis=1)
        CW = 512
        for c in range(W // CW):
            gh, gl = split3(g_ref[pl.ds(k0, B), CW * c:CW * (c + 1)])
            u = jnp.dot(lcat, jnp.concatenate([gh, gh, gl], axis=0), preferred_element_type=f32)
            uh, ul = split3(u)
            ur_ref[0:B, CW * c:CW * (c + 1)] = uh
            ur_ref[B:2 * B, CW * c:CW * (c + 1)] = uh
            ur_ref[2 * B:, CW * c:CW * (c + 1)] = ul
            if c < N // CW:
                for t in range(CW // B):
                    ut = u[:, B * t:B * (t + 1)].T
                    th, tl = split3(ut)
                    r0 = CW * c + B * t
                    ul_ref[r0:r0 + B, 0:B] = th
                    ul_ref[r0:r0 + B, B:2 * B] = tl
                    ul_ref[r0:r0 + B, 2 * B:] = th
            else:
                var_ref[...] += jnp.sum(u * u, axis=0, keepdims=True)

        @pl.loop(k + 1, NB)
        def _(i):
            i0 = pl.multiple_of(i * B, B)
            lhs = ul_ref[pl.ds(i0, B), :]
            for c in range(W // CW):
                d = jnp.dot(lhs, ur_ref[:, CW * c:CW * (c + 1)], preferred_element_type=f32)
                g_ref[pl.ds(i0, B), CW * c:CW * (c + 1)] -= d
    var_ref[...] = var_ref[...] * (4.0 / N)


def chol_var(a, prior, ft):
    return pl.pallas_call(
        chol_kernel,
        out_shape=jax.ShapeDtypeStruct((1, R_), f32),
        in_specs=[pl.BlockSpec(memory_space=pltpu.VMEM)] * 3,
        out_specs=pl.BlockSpec(memory_space=pltpu.VMEM),
        scratch_shapes=[
            pltpu.VMEM((N, W), f32),
            pltpu.VMEM((B, B), f32),
            pltpu.VMEM((N, 3 * B), bf16),
            pltpu.VMEM((3 * B, W), bf16),
        ],
        compiler_params=pltpu.CompilerParams(vmem_limit_bytes=48 * 1024 * 1024),
    )(a, prior, ft)


MESH = pl.DeviceIdType.MESH
C = 14
KB = 256


def gather_kernel(hid_ref, proj_ref, hw_ref, hb_ref, lab_ref, cw_ref, ft_ref, gram_ref, log_ref,
                  h_ref, buf_ref, acc_ref, wt_ref, loc_sem, send_sem, recv_sem):
    m = lax.axis_index("member")
    d = lax.axis_index("dp")
    c = lax.rem(d, 2)
    x = lax.rem(d // 2, 4)
    yh = d // 8

    def dp(dy, dx, t):
        yy = yh if dy == 0 else 1 - yh
        cc = c if t == 0 else 1 - c
        return (yy * 4 + lax.rem(x + dx, 4)) * 2 + cc

    to_r, to_l, to_y, to_m = dp(0, 1, 0), dp(0, 3, 0), dp(1, 0, 0), dp(0, 0, 1)
    me = d
    own_copy = pltpu.make_async_copy(proj_ref, buf_ref.at[me], loc_sem.at[0])
    own_copy.start()
    hid_copy = pltpu.make_async_copy(hid_ref, h_ref, loc_sem.at[1])
    hid_copy.start()
    bar = pltpu.get_barrier_semaphore()
    for t in (to_r, to_l, to_y, to_m):
        pl.semaphore_signal(bar, inc=1, device_id=(m, t), device_id_type=MESH)
    pl.semaphore_wait(bar, 4)
    own_copy.wait()
    sends = []

    def half(s, h):
        return buf_ref.at[s, pl.ds(h * (KB // 2), KB // 2), :]

    def copy(s, h, to, i):
        return pltpu.make_async_remote_copy(
            src_ref=half(s, h), dst_ref=half(s, h), send_sem=send_sem.at[i], recv_sem=recv_sem.at[s, h],
            device_id=(m, to), device_id_type=MESH)

    def send(to, s, h):
        cp = copy(s, h, to, len(sends))
        cp.start()
        sends.append(cp)

    def wait(s, h):
        copy(s, h, to_m, 0).wait_recv()

    def mm(s, first=False):
        k0 = pl.multiple_of(s * KB, KB)

        @pl.loop(0, P_SIZE // 256)
        def _(n):
            n0 = pl.multiple_of(n * 256, 256)
            r = jnp.dot(h_ref[:, pl.ds(k0, KB)], buf_ref[s, :, pl.ds(n0, 256)], preferred_element_type=f32)
            if first:
                acc_ref[:, pl.ds(n0, 256)] = r
            else:
                acc_ref[:, pl.ds(n0, 256)] += r

    send(to_r, me, 0)
    send(to_l, me, 1)
    send(to_y, me, 0)
    send(to_y, me, 1)
    send(to_r, me, 1)
    send(to_l, me, 0)
    send(to_m, me, 0)
    send(to_m, me, 1)
    hid_copy.wait()
    mm(me, True)
    mate = dp(0, 0, 1)
    wait(mate, 0)
    wait(mate, 1)
    mm(mate)
    left, right, anti, part = dp(0, 3, 0), dp(0, 1, 0), dp(0, 2, 0), dp(1, 0, 0)
    wait(left, 0)
    send(to_r, left, 0)
    wait(right, 1)
    send(to_l, right, 1)
    send(to_m, left, 0)
    send(to_m, right, 1)
    for h in (0, 1):
        wait(part, h)
        send(to_r, part, h)
        send(to_l, part, h)
        send(to_m, part, h)
    wait(left, 1)
    send(to_m, left, 1)
    wait(right, 0)
    send(to_m, right, 0)
    mm(left)
    mm(right)
    for h in (0, 1):
        wait(anti, h)
        send(to_y, anti, h)
        send(to_m, anti, h)
    mm(part)
    for s in (dp(0, 3, 1), dp(0, 1, 1), dp(1, 0, 1)):
        wait(s, 0)
        wait(s, 1)
        mm(s)
    mm(anti)
    s = dp(0, 2, 1)
    wait(s, 0)
    wait(s, 1)
    mm(s)
    pl_, pr, pa = dp(1, 3, 0), dp(1, 1, 0), dp(1, 2, 0)
    for h in (0, 1):
        wait(pl_, h)
        send(to_m, pl_, h)
        wait(pr, h)
        send(to_m, pr, h)
    mm(pl_)
    mm(pr)
    for h in (0, 1):
        wait(pa, h)
        send(to_m, pa, h)
    mm(pa)
    for s in (dp(1, 3, 1), dp(1, 1, 1), dp(1, 2, 1)):
        wait(s, 0)
        wait(s, 1)
        mm(s)

    for j in range(NB):
        ft_ref[B * j:B * (j + 1), :] = acc_ref[:, B * j:B * (j + 1)].T.astype(bf16)
    logits = jnp.dot(hw_ref[...], ft_ref[...], preferred_element_type=f32) + hb_ref[...]
    log_ref[...] = logits
    cat = lax.broadcasted_iota(jnp.int32, (C, R_), 0)
    row_weight = jnp.sum(jnp.where(cat == lab_ref[...], cw_ref[...].astype(f32), f32(0)), axis=0, keepdims=True)
    expo = jnp.exp(logits)
    probs = expo / jnp.sum(expo, axis=0, keepdims=True)
    curv = row_weight * (1.0 - jnp.sum(probs * probs, axis=0, keepdims=True))
    root = jnp.sqrt(curv)
    for j in range(NB):
        wt_ref[B * j:B * (j + 1), :] = (ft_ref[B * j:B * (j + 1), :].astype(f32) * root).astype(bf16)
    for i in range(4):
        gram_ref[256 * i:256 * (i + 1), 256 * i:] = lax.dot_general(
            wt_ref[256 * i:256 * (i + 1), :], wt_ref[256 * i:, :], (((1,), (1,)), ((), ())), preferred_element_type=f32)
    for cp in sends:
        cp.wait_send()


def gather_features(hidden, proj, hw, hb, labels, cw):
    vm = pl.BlockSpec(memory_space=pltpu.VMEM)
    any_ = pl.BlockSpec(memory_space=pl.ANY)
    return pl.pallas_call(
        gather_kernel,
        out_shape=(
            jax.ShapeDtypeStruct((N, R_), bf16),
            jax.ShapeDtypeStruct((N, N), f32),
            jax.ShapeDtypeStruct((C, R_), f32),
        ),
        in_specs=[any_, any_, vm, vm, vm, vm],
        out_specs=(vm, vm, vm),
        scratch_shapes=[
            pltpu.VMEM((R_, 4096), bf16),
            pltpu.VMEM((16, KB, P_SIZE), bf16),
            pltpu.VMEM((R_, P_SIZE), f32),
            pltpu.VMEM((N, R_), bf16),
            pltpu.SemaphoreType.DMA((2,)),
            pltpu.SemaphoreType.DMA((30,)),
            pltpu.SemaphoreType.DMA((16, 2)),
        ],
        compiler_params=pltpu.CompilerParams(
            collective_id=0, has_side_effects=True, vmem_limit_bytes=48 * 1024 * 1024),
    )(hidden, proj, hw, hb, labels, cw)


def body(hidden, projection, head_weight, head_bias, prior_precision, labels, category_weight):
    ft, gram_part, logits = gather_features(
        hidden[0], projection[0], head_weight[0], head_bias[0][:, None], labels[None, :], category_weight[:, None])
    gram = lax.psum(gram_part, "dp")
    variance = chol_var(gram, prior_precision, ft)[0]
    scaled = logits / jnp.sqrt(1.0 + variance)[None, :]
    moder = jnp.exp(scaled)
    moder = moder / jnp.sum(moder, axis=0, keepdims=True)
    summed = lax.psum(moder, "member")
    ensemble = summed / lax.axis_size("member")
    return (variance[None, :], ensemble)


def solution(mesh):
    return jax.shard_map(
        body,
        mesh=mesh,
        in_specs=(
            P("member", "dp", None),
            P("member", "dp", None),
            P("member", None, None),
            P("member", None),
            P("member", None),
            P("dp"),
            P(),
        ),
        out_specs=(P("member", "dp"), P(None, "dp")),
        check_vma=False,
    )
```

```python
import jax, jax.numpy as jnp
from jax import lax
from jax.experimental import pallas as pl
from jax.experimental.pallas import tpu as pltpu
from jax.sharding import PartitionSpec as P

N = 1024
P_SIZE = 1024
ROWS = 8192
B = 128
NB = N // B
R_ = 512
W = N + R_
f32 = jnp.float32
bf16 = jnp.bfloat16


def split3(x):
    hi = x.astype(bf16)
    lo = (x - hi.astype(f32)).astype(bf16)
    return hi, lo


def diag_inverse(S):
    G = 8
    n = B // G
    R = list(S)
    lane = lax.broadcasted_iota(jnp.int32, (G, B), 1)
    sub = lax.broadcasted_iota(jnp.int32, (G, B), 0)
    Q = [jnp.where(lane == sub + G * i, f32(1), f32(0)) for i in range(n)]
    out = [None] * n
    for b in range(n):
        c = [[jnp.broadcast_to(R[i][:, G * b + k:G * b + k + 1], (G, B)) for k in range(G)] for i in range(b, n)]
        cb = c[0]
        rb, qb = R[b], Q[b]
        dv = jnp.ones((G, B), f32)
        inv, rj, qj, cs = [], [], [], []
        for j in range(G):
            p = jnp.broadcast_to(cb[j][j:j + 1, :], (G, B))
            iv = 1.0 / p
            dv = jnp.where(sub == j, p, dv)
            m = jnp.where(sub > j, cb[j] * iv, f32(0))
            row = [None] * G
            for k in range(j + 1, G):
                row[k] = jnp.broadcast_to(cb[k][j:j + 1, :], (G, B))
                cb[k] = cb[k] - m * row[k]
            r = jnp.broadcast_to(rb[j:j + 1, :], (G, B))
            q = jnp.broadcast_to(qb[j:j + 1, :], (G, B))
            if j < G - 1:
                rb = rb - m * r
                qb = qb - m * q
            inv.append(iv); rj.append(r); qj.append(q); cs.append(row)
        out[b] = qb * lax.rsqrt(dv)
        for i in range(b + 1, n):
            ci = c[i - b]
            ri, qi = R[i], Q[i]
            for j in range(G):
                m = ci[j] * inv[j]
                for k in range(j + 1, G):
                    ci[k] = ci[k] - m * cs[j][k]
                ri = ri - m * rj[j]
                qi = qi - m * qj[j]
            R[i], Q[i] = ri, qi
    return out


MESH = pl.DeviceIdType.MESH
C = 14
MEMBERS = 8
KB = 256


def laplace_kernel(hid_ref, proj_ref, hw_ref, hb_ref, prior_ref, lab_ref, cw_ref, var_ref, ens_ref,
                   h_ref, buf_ref, acc_ref, ft_ref, wt_ref, gp_ref, mate_ref, part_ref, a_ref,
                   g_ref, linv_ref, ul_ref, ur_ref, mod_ref, got_ref,
                   loc_sem, send_sem, recv_sem, ms_sem, mr_sem, ss_sem, sr_sem, gs_sem, gr_sem, fs_sem, fr_sem,
                   es_sem, er_sem):
    m = lax.axis_index("member")
    d = lax.axis_index("dp")
    c = lax.rem(d, 2)
    x = lax.rem(d // 2, 4)
    yh = d // 8

    def dp(dy, dx, t):
        yy = yh if dy == 0 else 1 - yh
        cc = c if t == 0 else 1 - c
        return (yy * 4 + lax.rem(x + dx, 4)) * 2 + cc

    to_r, to_l, to_y, to_m = dp(0, 1, 0), dp(0, 3, 0), dp(1, 0, 0), dp(0, 0, 1)
    me = d
    own_copy = pltpu.make_async_copy(proj_ref, buf_ref.at[me], loc_sem.at[0])
    own_copy.start()
    hid_copy = pltpu.make_async_copy(hid_ref, h_ref, loc_sem.at[1])
    hid_copy.start()
    bar = pltpu.get_barrier_semaphore()
    chip = d // 2
    peers = [lax.rem(chip + rel, 8) * 2 + c for rel in range(1, 8)]
    for t in peers + [to_m]:
        pl.semaphore_signal(bar, inc=1, device_id=(m, t), device_id_type=MESH)
    members = [lax.rem(m + rel, MEMBERS) for rel in range(1, MEMBERS)]
    for t in members:
        pl.semaphore_signal(bar, inc=1, device_id=(t, d), device_id_type=MESH)
    pl.semaphore_wait(bar, 15)
    own_copy.wait()
    sends = []

    def half(s, h):
        return buf_ref.at[s, pl.ds(h * (KB // 2), KB // 2), :]

    def copy(s, h, to, i):
        return pltpu.make_async_remote_copy(
            src_ref=half(s, h), dst_ref=half(s, h), send_sem=send_sem.at[i], recv_sem=recv_sem.at[s, h],
            device_id=(m, to), device_id_type=MESH)

    def send(to, s, h):
        cp = copy(s, h, to, len(sends))
        cp.start()
        sends.append(cp)

    def wait(s, h):
        copy(s, h, to_m, 0).wait_recv()

    def mm(s, first=False):
        k0 = pl.multiple_of(s * KB, KB)

        @pl.loop(0, P_SIZE // 256)
        def _(n):
            n0 = pl.multiple_of(n * 256, 256)
            r = jnp.dot(h_ref[:, pl.ds(k0, KB)], buf_ref[s, :, pl.ds(n0, 256)], preferred_element_type=f32)
            if first:
                acc_ref[:, pl.ds(n0, 256)] = r
            else:
                acc_ref[:, pl.ds(n0, 256)] += r

    send(to_r, me, 0)
    send(to_l, me, 1)
    send(to_y, me, 0)
    send(to_y, me, 1)
    send(to_r, me, 1)
    send(to_l, me, 0)
    send(to_m, me, 0)
    send(to_m, me, 1)
    hid_copy.wait()
    mm(me, True)
    mate = dp(0, 0, 1)
    wait(mate, 0)
    wait(mate, 1)
    mm(mate)
    left, right, anti, part = dp(0, 3, 0), dp(0, 1, 0), dp(0, 2, 0), dp(1, 0, 0)
    wait(left, 0)
    send(to_r, left, 0)
    wait(right, 1)
    send(to_l, right, 1)
    send(to_m, left, 0)
    send(to_m, right, 1)
    for h in (0, 1):
        wait(part, h)
        send(to_r, part, h)
        send(to_l, part, h)
        send(to_m, part, h)
    wait(left, 1)
    send(to_m, left, 1)
    wait(right, 0)
    send(to_m, right, 0)
    mm(left)
    mm(right)
    for h in (0, 1):
        wait(anti, h)
        send(to_y, anti, h)
        send(to_m, anti, h)
    mm(part)
    for s in (dp(0, 3, 1), dp(0, 1, 1), dp(1, 0, 1)):
        wait(s, 0)
        wait(s, 1)
        mm(s)
    mm(anti)
    s = dp(0, 2, 1)
    wait(s, 0)
    wait(s, 1)
    mm(s)
    pl_, pr, pa = dp(1, 3, 0), dp(1, 1, 0), dp(1, 2, 0)
    for h in (0, 1):
        wait(pl_, h)
        send(to_m, pl_, h)
        wait(pr, h)
        send(to_m, pr, h)
    mm(pl_)
    mm(pr)
    for h in (0, 1):
        wait(pa, h)
        send(to_m, pa, h)
    mm(pa)
    for s in (dp(1, 3, 1), dp(1, 1, 1), dp(1, 2, 1)):
        wait(s, 0)
        wait(s, 1)
        mm(s)

    for j in range(NB):
        ft_ref[B * j:B * (j + 1), :] = acc_ref[:, B * j:B * (j + 1)].T.astype(bf16)
    logits = jnp.dot(hw_ref[...], ft_ref[...], preferred_element_type=f32) + hb_ref[...]
    cat = lax.broadcasted_iota(jnp.int32, (C, R_), 0)
    row_weight = jnp.sum(jnp.where(cat == lab_ref[...], cw_ref[...].astype(f32), f32(0)), axis=0, keepdims=True)
    expo = jnp.exp(logits)
    probs = expo / jnp.sum(expo, axis=0, keepdims=True)
    curv = row_weight * (1.0 - jnp.sum(probs * probs, axis=0, keepdims=True))
    root = jnp.sqrt(curv)
    for j in range(NB):
        wt_ref[B * j:B * (j + 1), :] = (ft_ref[B * j:B * (j + 1), :].astype(f32) * root).astype(bf16)

    H = B // 2
    mine = pl.multiple_of(c * H, H)
    other = pl.multiple_of((1 - c) * H, H)

    def mate_copy(i):
        return pltpu.make_async_remote_copy(
            src_ref=gp_ref.at[pl.ds(B * i + other, H), pl.ds(B * i, N - B * i)],
            dst_ref=mate_ref.at[i, :, pl.ds(B * i, N - B * i)],
            send_sem=ms_sem.at[i], recv_sem=mr_sem.at[i], device_id=(m, to_m), device_id_type=MESH)

    def part_copy(i, rel):
        to = lax.rem(chip + rel, 8)
        return pltpu.make_async_remote_copy(
            src_ref=gp_ref.at[pl.ds(pl.multiple_of(B * i + mine + 8 * to, 8), 8), pl.ds(B * i, N - B * i)],
            dst_ref=part_ref.at[i, pl.ds(8 * (rel - 1), 8), pl.ds(B * i, N - B * i)],
            send_sem=ss_sem.at[i], recv_sem=sr_sem.at[i], device_id=(m, to * 2 + c), device_id_type=MESH)

    def part_all(i):
        ref = part_ref.at[i, :, pl.ds(B * i, N - B * i)]
        return pltpu.make_async_remote_copy(
            src_ref=ref, dst_ref=ref, send_sem=ss_sem.at[i], recv_sem=sr_sem.at[i], device_id=(m, to_m), device_id_type=MESH)

    def row_copy(i, rel):
        ref = a_ref.at[pl.ds(pl.multiple_of(B * i + mine + 8 * chip, 8), 8), pl.ds(B * i, N - B * i)]
        return pltpu.make_async_remote_copy(
            src_ref=ref, dst_ref=ref, send_sem=gs_sem.at[i], recv_sem=gr_sem.at[i],
            device_id=(m, lax.rem(chip + rel, 8) * 2 + c), device_id_type=MESH)

    def row_all(i):
        ref = a_ref.at[pl.ds(pl.multiple_of(B * i + mine, 8), H - 8), pl.ds(B * i, N - B * i)]
        return pltpu.make_async_remote_copy(
            src_ref=ref, dst_ref=ref, send_sem=gs_sem.at[i], recv_sem=gr_sem.at[i], device_id=(m, to_m), device_id_type=MESH)

    def forward_copy(i):
        ref = a_ref.at[pl.ds(pl.multiple_of(B * i + mine, H), H), pl.ds(B * i, N - B * i)]
        return pltpu.make_async_remote_copy(
            src_ref=ref, dst_ref=ref, send_sem=fs_sem.at[i], recv_sem=fr_sem.at[i], device_id=(m, to_m), device_id_type=MESH)

    def scatter(i):
        mate_copy(i).wait_recv()
        rows = pl.ds(pl.multiple_of(B * i + mine, H), H)
        gp_ref[rows, B * i:] += mate_ref[i, :, B * i:]
        for rel in range(1, 8):
            part_copy(i, rel).start()

    def reduce(i):
        part_all(i).wait_recv()
        rows = pl.ds(pl.multiple_of(B * i + mine + 8 * chip, 8), 8)
        total = gp_ref[rows, B * i:]
        for rel in range(1, 8):
            total += part_ref[i, 8 * (rel - 1):8 * rel, B * i:]
        a_ref[rows, B * i:] = total
        for rel in range(1, 8):
            row_copy(i, rel).start()

    def forward(i):
        row_all(i).wait_recv()
        forward_copy(i).start()

    for i in range(NB):
        gp_ref[B * i:B * (i + 1), B * i:] = lax.dot_general(
            wt_ref[B * i:B * (i + 1), :], wt_ref[B * i:, :], (((1,), (1,)), ((), ())), preferred_element_type=f32)
        mate_copy(i).start()
    scatter(0)
    for i in range(NB):
        g_ref[B * i:B * (i + 1), :N] = jnp.zeros((B, N), f32)
        g_ref[B * i:B * (i + 1), N:] = ft_ref[B * i:B * (i + 1), :].astype(f32)
    reduce(0)
    scatter(1)
    scatter(2)
    forward(0)
    var_ref[...] = jnp.zeros_like(var_ref)
    diag_r = lax.broadcasted_iota(jnp.int32, (8, B), 0)
    diag_c = lax.broadcasted_iota(jnp.int32, (8, B), 1)
    CW = 512

    @pl.loop(0, NB)
    def _(k):
        k0 = pl.multiple_of(k * B, B)
        for i in range(NB):
            @pl.when(k == i)
            def _(i=i):
                forward_copy(i).wait_recv()
                if i + 1 < NB:
                    reduce(i + 1)
                if i + 3 < NB:
                    scatter(i + 3)
        pr = prior_ref[:, pl.ds(k0, B)]
        S = []
        for i in range(16):
            rows = pl.ds(k0 + 8 * i, 8)
            s = g_ref[rows, pl.ds(k0, B)] + a_ref[rows, pl.ds(k0, B)] * f32(1.0 / ROWS)
            S.append(s + jnp.where(diag_c == diag_r + 8 * i, pr, f32(0)))
        out = diag_inverse(S)
        for i in range(16):
            linv_ref[pl.ds(8 * i, 8), :] = out[i]
        for i in range(NB - 1):
            @pl.when(k == i)
            def _(i=i):
                forward(i + 1)
        lh, ll = split3(linv_ref[...])
        lcat = jnp.concatenate([lh, ll, lh], axis=1)

        def row_panel(c0, with_a):
            g = g_ref[pl.ds(k0, B), c0:c0 + CW]
            if with_a:
                g = g + a_ref[pl.ds(k0, B), c0:c0 + CW] * f32(1.0 / ROWS)
            gh, gl = split3(g)
            u = jnp.dot(lcat, jnp.concatenate([gh, gh, gl], axis=0), preferred_element_type=f32)
            uh, ul = split3(u)
            ur_ref[0:B, c0:c0 + CW] = uh
            ur_ref[B:2 * B, c0:c0 + CW] = uh
            ur_ref[2 * B:, c0:c0 + CW] = ul
            if with_a:
                for t in range(CW // B):
                    th, tl = split3(u[:, B * t:B * (t + 1)].T)
                    r0 = c0 + B * t
                    ul_ref[r0:r0 + B, 0:B] = th
                    ul_ref[r0:r0 + B, B:2 * B] = tl
                    ul_ref[r0:r0 + B, 2 * B:] = th
            else:
                var_ref[...] += jnp.sum(u * u, axis=0, keepdims=True)

        row_panel(N, False)

        @pl.when(k < NB - 1)
        def _():
            row_panel(CW, True)

        @pl.when(k < NB // 2 - 1)
        def _():
            row_panel(0, True)

        @pl.loop(k + 1, NB)
        def _(i):
            i0 = pl.multiple_of(i * B, B)
            lhs = ul_ref[pl.ds(i0, B), :]

            def update(c0):
                g_ref[pl.ds(i0, B), c0:c0 + CW] -= jnp.dot(lhs, ur_ref[:, c0:c0 + CW], preferred_element_type=f32)

            update(N)
            update(CW)

            @pl.when(i < NB // 2)
            def _():
                update(0)

    var = var_ref[...] * (4.0 / P_SIZE)
    var_ref[...] = var
    moder = jnp.exp(logits / jnp.sqrt(1.0 + var))
    moder = moder / jnp.sum(moder, axis=0, keepdims=True)
    mod_ref[0:C, :] = moder

    def member_copy(rel):
        return pltpu.make_async_remote_copy(
            src_ref=mod_ref, dst_ref=got_ref.at[rel - 1], send_sem=es_sem, recv_sem=er_sem,
            device_id=(members[rel - 1], d), device_id_type=MESH)

    for rel in range(1, MEMBERS):
        member_copy(rel).start()
    for i in range(NB):
        mate_copy(i).wait_send()
        part_all(i).wait_send()
        row_all(i).wait_send()
        forward_copy(i).wait_send()
    every = pltpu.make_async_remote_copy(
        src_ref=got_ref, dst_ref=got_ref, send_sem=es_sem, recv_sem=er_sem, device_id=(m, to_m), device_id_type=MESH)
    every.wait_recv()
    total = moder
    for rel in range(1, MEMBERS):
        total += got_ref[rel - 1, 0:C, :]
    ens_ref[...] = total * f32(1.0 / MEMBERS)
    every.wait_send()
    for cp in sends:
        cp.wait_send()


def laplace(hidden, proj, hw, hb, prior, labels, cw):
    vm = pl.BlockSpec(memory_space=pltpu.VMEM)
    any_ = pl.BlockSpec(memory_space=pl.ANY)
    dma = pltpu.SemaphoreType.DMA
    return pl.pallas_call(
        laplace_kernel,
        out_shape=(jax.ShapeDtypeStruct((1, R_), f32), jax.ShapeDtypeStruct((C, R_), f32)),
        in_specs=[any_, any_, vm, vm, vm, vm, vm],
        out_specs=(vm, vm),
        scratch_shapes=[
            pltpu.VMEM((R_, 4096), bf16),
            pltpu.VMEM((16, KB, P_SIZE), bf16),
            pltpu.VMEM((R_, P_SIZE), f32),
            pltpu.VMEM((N, R_), bf16),
            pltpu.VMEM((N, R_), bf16),
            pltpu.VMEM((N, N), f32),
            pltpu.VMEM((NB, B // 2, N), f32),
            pltpu.VMEM((NB, 56, N), f32),
            pltpu.VMEM((N, N), f32),
            pltpu.VMEM((N, W), f32),
            pltpu.VMEM((B, B), f32),
            pltpu.VMEM((N, 3 * B), bf16),
            pltpu.VMEM((3 * B, W), bf16),
            pltpu.VMEM((16, R_), f32),
            pltpu.VMEM((MEMBERS - 1, 16, R_), f32),
            dma((2,)), dma((30,)), dma((16, 2)),
            dma((NB,)), dma((NB,)), dma((NB,)), dma((NB,)), dma((NB,)), dma((NB,)), dma((NB,)), dma((NB,)),
            dma, dma,
        ],
        compiler_params=pltpu.CompilerParams(
            collective_id=0, has_side_effects=True, vmem_limit_bytes=56 * 1024 * 1024),
    )(hidden, proj, hw, hb, prior, labels, cw)


def body(hidden, projection, head_weight, head_bias, prior_precision, labels, category_weight):
    return laplace(
        hidden[0], projection[0], head_weight[0], head_bias[0][:, None], prior_precision,
        labels[None, :], category_weight[:, None])


def solution(mesh):
    return jax.shard_map(
        body,
        mesh=mesh,
        in_specs=(
            P("member", "dp", None),
            P("member", "dp", None),
            P("member", None, None),
            P("member", None),
            P("member", None),
            P("dp"),
            P(),
        ),
        out_specs=(P("member", "dp"), P(None, "dp")),
        check_vma=False,
    )
```

```python
import jax, jax.numpy as jnp
from jax import lax
from jax.experimental import pallas as pl
from jax.experimental.pallas import tpu as pltpu
from jax.sharding import PartitionSpec as P

N = 1024
P_SIZE = 1024
ROWS = 8192
B = 128
NB = N // B
R_ = 512
W = N + R_
f32 = jnp.float32
bf16 = jnp.bfloat16


def split3(x):
    hi = x.astype(bf16)
    lo = (x - hi.astype(f32)).astype(bf16)
    return hi, lo


def diag_inverse(S):
    G = 8
    n = B // G
    T = list(S)
    lane = lax.broadcasted_iota(jnp.int32, (G, B), 1)
    sub = lax.broadcasted_iota(jnp.int32, (G, B), 0)
    out = [None] * n

    def column(t, j):
        return jnp.take_along_axis(t, jnp.full((G, B), j, jnp.int32), axis=1)

    def row(t, j):
        return jnp.broadcast_to(t[j:j + 1, :], (G, B))

    for b in range(n):
        cb = [column(T[b], G * b + k) for k in range(G)]
        below = range(b + 1, n)
        cn = {i: [column(T[i], G * b + k) for k in range(G)] for i in below}
        own = (lane >= G * b) & (lane < G * b + G)
        tn = {i: jnp.where(own, f32(0), T[i]) for i in below}
        rb = T[b]
        qb = jnp.where(lane < G * b, rb, jnp.where(lane == sub + G * b, f32(1), f32(0)))
        dv = jnp.ones((G, B), f32)
        for j in range(G):
            p = row(cb[j], j)
            inv = 1.0 / p
            dv = jnp.where(sub == j, p, dv)
            m = jnp.where(sub > j, cb[j] * inv, f32(0))
            mn = {i: cn[i][j] * inv for i in below}
            for k in range(j + 1, G):
                r = row(cb[k], j)
                cb[k] = cb[k] - m * r
                for i in below:
                    cn[i][k] = cn[i][k] - mn[i] * r
            q = row(qb, j)
            if b < n - 1:
                r = row(rb, j)
                full = jnp.where(lane < G * b + G, q, r)
                for i in below:
                    tn[i] = tn[i] - mn[i] * full
                if j < G - 1:
                    rb = rb - m * r
            if j < G - 1:
                qb = qb - m * q
        out[b] = qb * lax.rsqrt(dv)
        for i in below:
            T[i] = tn[i]
    return out


MESH = pl.DeviceIdType.MESH
C = 14
MEMBERS = 8
GROUPS = ((0, 1, 0, 128), (0, 1, 128, 896), (1, 1, 128, 896), (2, 2, 256, 768), (4, 4, 512, 512))
KB = 256
MN = 512


def laplace_kernel(hid_ref, proj_ref, hw_ref, hb_ref, prior_ref, lab_ref, cw_ref, out_ref,
                   h_ref, buf_ref, acc_ref, ft_ref, wt_ref, gp_ref, mate_ref, part_ref, a_ref, var_ref,
                   g_ref, linv_ref, ul_ref, ur_ref, mod_ref, got_ref,
                   loc_sem, send_sem, recv_sem, ms_sem, mr_sem, ss_sem, sr_sem, gs_sem, gr_sem, fs_sem, fr_sem,
                   es_sem, er_sem):
    m = lax.axis_index("member")
    d = lax.axis_index("dp")
    c = lax.rem(d, 2)
    x = lax.rem(d // 2, 4)
    yh = d // 8

    def dp(dy, dx, t):
        yy = yh if dy == 0 else 1 - yh
        cc = c if t == 0 else 1 - c
        return (yy * 4 + lax.rem(x + dx, 4)) * 2 + cc

    to_r, to_l, to_y, to_m = dp(0, 1, 0), dp(0, 3, 0), dp(1, 0, 0), dp(0, 0, 1)
    me = d
    own_copy = pltpu.make_async_copy(proj_ref, buf_ref.at[d // 2, pl.ds(pl.multiple_of(c * KB, KB), KB), :], loc_sem.at[0])
    own_copy.start()
    hid_copy = pltpu.make_async_copy(hid_ref, h_ref, loc_sem.at[1])
    hid_copy.start()
    bar = pltpu.get_barrier_semaphore()
    chip = d // 2
    peers = [lax.rem(chip + rel, 8) * 2 + c for rel in range(1, 8)]
    for t in peers + [to_m]:
        pl.semaphore_signal(bar, inc=1, device_id=(m, t), device_id_type=MESH)
    members = [lax.rem(m + rel, MEMBERS) for rel in range(1, MEMBERS)]
    for t in members:
        pl.semaphore_signal(bar, inc=1, device_id=(t, d), device_id_type=MESH)
    pl.semaphore_wait(bar, 15)
    own_copy.wait()
    sends = []

    def half(s, h):
        return buf_ref.at[s // 2, pl.ds(pl.multiple_of(lax.rem(s, 2) * KB + h * (KB // 2), KB // 2), KB // 2), :]

    def copy(s, h, to, i):
        return pltpu.make_async_remote_copy(
            src_ref=half(s, h), dst_ref=half(s, h), send_sem=send_sem.at[i], recv_sem=recv_sem.at[s, h],
            device_id=(m, to), device_id_type=MESH)

    def send(to, s, h):
        cp = copy(s, h, to, len(sends))
        cp.start()
        sends.append(cp)

    def wait(s, h):
        copy(s, h, to_m, 0).wait_recv()

    def mm(s, first=False):
        place = s // 2
        k0 = pl.multiple_of(place * 2 * KB, 2 * KB)

        @pl.loop(0, P_SIZE // MN)
        def _(n):
            n0 = pl.multiple_of(n * MN, MN)
            r = jnp.dot(h_ref[:, pl.ds(k0, 2 * KB)], buf_ref[place, :, pl.ds(n0, MN)], preferred_element_type=f32)
            if first:
                acc_ref[:, pl.ds(n0, MN)] = r
            else:
                acc_ref[:, pl.ds(n0, MN)] += r

    left, right, anti, part = dp(0, 3, 0), dp(0, 1, 0), dp(0, 2, 0), dp(1, 0, 0)
    far_l, far_r, far_a = dp(1, 3, 0), dp(1, 1, 0), dp(1, 2, 0)

    def mate_mm(dy, dx, first=False):
        s = dp(dy, dx, 1)
        wait(s, 0)
        wait(s, 1)
        mm(s, first)

    send(to_r, me, 0)
    send(to_l, me, 1)
    send(to_y, me, 0)
    send(to_y, me, 1)
    send(to_r, me, 1)
    send(to_l, me, 0)
    send(to_m, me, 0)
    send(to_m, me, 1)
    for i in range(NB):
        g_ref[B * i:B * (i + 1), :N] = jnp.zeros((B, N), f32)
    hid_copy.wait()
    wait(left, 0)
    send(to_r, left, 0)
    send(to_y, left, 0)
    wait(right, 1)
    send(to_l, right, 1)
    send(to_y, right, 1)
    send(to_m, left, 0)
    send(to_m, right, 1)
    wait(part, 0)
    send(to_l, part, 0)
    wait(part, 1)
    send(to_r, part, 1)
    send(to_m, part, 0)
    send(to_m, part, 1)
    wait(left, 1)
    send(to_m, left, 1)
    wait(right, 0)
    send(to_m, right, 0)
    mate_mm(0, 0, True)
    mate_mm(0, 3)
    mate_mm(0, 1)
    wait(anti, 0)
    send(to_m, anti, 0)
    wait(anti, 1)
    send(to_m, anti, 1)
    wait(far_l, 0)
    send(to_r, far_l, 0)
    wait(far_r, 1)
    send(to_l, far_r, 1)
    send(to_m, far_l, 0)
    send(to_m, far_r, 1)
    mate_mm(1, 0)
    mate_mm(0, 2)
    wait(far_l, 1)
    send(to_m, far_l, 1)
    wait(far_r, 0)
    send(to_m, far_r, 0)
    mate_mm(1, 3)
    mate_mm(1, 1)
    wait(far_a, 0)
    send(to_m, far_a, 0)
    wait(far_a, 1)
    send(to_m, far_a, 1)
    mate_mm(1, 2)

    for j in range(NB):
        ft_ref[B * j:B * (j + 1), :] = acc_ref[:, B * j:B * (j + 1)].T.astype(bf16)
    eye = lax.broadcasted_iota(jnp.int32, (C, C), 0) == lax.broadcasted_iota(jnp.int32, (C, C), 1)
    bias = jnp.sum(jnp.where(eye, hb_ref[...], f32(0)), axis=1, keepdims=True)
    weight = jnp.sum(jnp.where(eye, cw_ref[...].astype(f32), f32(0)), axis=1, keepdims=True)
    logits = jnp.dot(hw_ref[...], ft_ref[...], preferred_element_type=f32) + bias
    cat = lax.broadcasted_iota(jnp.int32, (C, R_), 0)
    row_weight = jnp.sum(jnp.where(cat == lab_ref[...], weight, f32(0)), axis=0, keepdims=True)
    expo = jnp.exp(logits)
    probs = expo / jnp.sum(expo, axis=0, keepdims=True)
    curv = row_weight * (1.0 - jnp.sum(probs * probs, axis=0, keepdims=True))
    root = jnp.sqrt(curv)
    for j in range(NB):
        wt_ref[B * j:B * (j + 1), :] = (ft_ref[B * j:B * (j + 1), :].astype(f32) * root).astype(bf16)

    H = B // 2
    mine = pl.multiple_of(c * H, H)
    other = pl.multiple_of((1 - c) * H, H)
    slice_at = pl.multiple_of(mine + 8 * chip, 8)

    def remote(src, dst, sems, g, to):
        return pltpu.make_async_remote_copy(
            src_ref=src, dst_ref=dst, send_sem=sems[0].at[g], recv_sem=sems[1].at[g], device_id=(m, to), device_id_type=MESH)

    def view(ref, g, row0, rows):
        p0, count, col0, width = GROUPS[g]
        return ref.at[pl.ds(p0, count), pl.ds(row0, rows), pl.ds(col0, width)]

    def mate_copy(g):
        return remote(view(gp_ref, g, other, H), view(mate_ref, g, 0, H), (ms_sem, mr_sem), g, to_m)

    def part_copy(g, rel):
        to = lax.rem(chip + rel, 8)
        return remote(view(gp_ref, g, pl.multiple_of(mine + 8 * to, 8), 8), view(part_ref, g, 8 * (rel - 1), 8),
                      (ss_sem, sr_sem), g, to * 2 + c)

    def part_all(g):
        return remote(view(part_ref, g, 0, 56), view(part_ref, g, 0, 56), (ss_sem, sr_sem), g, to_m)

    def row_copy(g, rel):
        ref = view(a_ref, g, slice_at, 8)
        return remote(ref, ref, (gs_sem, gr_sem), g, lax.rem(chip + rel, 8) * 2 + c)

    def row_all(g):
        ref = view(a_ref, g, mine, 56)
        return remote(ref, ref, (gs_sem, gr_sem), g, to_m)

    def forward_copy(g):
        ref = view(a_ref, g, mine, H)
        return remote(ref, ref, (fs_sem, fr_sem), g, to_m)

    def scatter(g):
        p0, count, col0, width = GROUPS[g]
        mate_copy(g).wait_recv()
        for p in range(p0, p0 + count):
            gp_ref[p, pl.ds(mine, H), col0:col0 + width] += mate_ref[p, :, col0:col0 + width]
        for rel in range(1, 8):
            part_copy(g, rel).start()

    def reduce(g):
        p0, count, col0, width = GROUPS[g]
        part_all(g).wait_recv()
        for p in range(p0, p0 + count):
            total = gp_ref[p, pl.ds(slice_at, 8), col0:col0 + width]
            for rel in range(1, 8):
                total += part_ref[p, 8 * (rel - 1):8 * rel, col0:col0 + width]
            a_ref[p, pl.ds(slice_at, 8), col0:col0 + width] = total
        for rel in range(1, 8):
            row_copy(g, rel).start()

    def forward(g):
        row_all(g).wait_recv()
        forward_copy(g).start()

    for g, (p0, count, col0, width) in enumerate(GROUPS):
        for p in range(p0, p0 + count):
            gp_ref[p, :, col0:col0 + width] = lax.dot_general(
                wt_ref[B * p:B * (p + 1), :], wt_ref[col0:col0 + width, :], (((1,), (1,)), ((), ())), preferred_element_type=f32)
        mate_copy(g).start()
        if g == 1:
            scatter(0)
    scatter(1)
    reduce(0)
    for i in range(NB):
        g_ref[B * i:B * (i + 1), N:] = ft_ref[B * i:B * (i + 1), :].astype(f32)
    var_ref[...] = jnp.zeros_like(var_ref)
    forward(0)
    scatter(2)
    reduce(1)
    done = lambda g: forward_copy(g).wait_recv()
    at_start = {0: [(done, 0)], 1: [(done, 2), (reduce, 3), (scatter, 4)], 2: [(done, 3), (reduce, 4)], 3: [(forward, 4)], 4: [(done, 4)]}
    after_diag = {0: [(forward, 1), (reduce, 2), (scatter, 3)], 1: [(forward, 3)]}
    before_rows = {0: [(done, 1)]}
    after_rows = {0: [(forward, 2)]}

    def run(table, k):
        for key, steps in table.items():
            @pl.when(k == key)
            def _(steps=steps):
                for step, g in steps:
                    step(g)

    diag_r = lax.broadcasted_iota(jnp.int32, (8, B), 0)
    diag_c = lax.broadcasted_iota(jnp.int32, (8, B), 1)
    CW = 512

    @pl.loop(0, NB)
    def _(k):
        k0 = pl.multiple_of(k * B, B)
        run(at_start, k)
        pr = prior_ref[:, pl.ds(k0, B)]
        S = []
        for i in range(16):
            rows = pl.ds(k0 + 8 * i, 8)
            s = g_ref[rows, pl.ds(k0, B)] + a_ref[k, pl.ds(8 * i, 8), pl.ds(k0, B)] * f32(1.0 / ROWS)
            S.append(s + jnp.where(diag_c == diag_r + 8 * i, pr, f32(0)))
        out = diag_inverse(S)
        for i in range(16):
            linv_ref[pl.ds(8 * i, 8), :] = out[i]
        run(after_diag, k)
        lh, ll = split3(linv_ref[...])
        lcat = jnp.concatenate([lh, ll, lh], axis=1)

        def row_panel(c0, with_a):
            g = g_ref[pl.ds(k0, B), c0:c0 + CW]
            if with_a:
                g = g + a_ref[k, :, c0:c0 + CW] * f32(1.0 / ROWS)
            gh, gl = split3(g)
            u = jnp.dot(lcat, jnp.concatenate([gh, gh, gl], axis=0), preferred_element_type=f32)
            uh, ul = split3(u)
            ur_ref[0:B, c0:c0 + CW] = uh
            ur_ref[B:2 * B, c0:c0 + CW] = uh
            ur_ref[2 * B:, c0:c0 + CW] = ul
            if with_a:
                for t in range(CW // B):
                    th, tl = split3(u[:, B * t:B * (t + 1)].T)
                    r0 = c0 + B * t
                    ul_ref[r0:r0 + B, 0:B] = th
                    ul_ref[r0:r0 + B, B:2 * B] = tl
                    ul_ref[r0:r0 + B, 2 * B:] = th
            else:
                var_ref[...] += jnp.sum(u * u, axis=0, keepdims=True)

        row_panel(N, False)
        run(before_rows, k)

        @pl.when(k < NB - 1)
        def _():
            row_panel(CW, True)

        @pl.when(k < NB // 2 - 1)
        def _():
            row_panel(0, True)

        run(after_rows, k)

        @pl.loop(k + 1, NB)
        def _(i):
            i0 = pl.multiple_of(i * B, B)
            lhs = ul_ref[pl.ds(i0, B), :]

            def update(c0):
                g_ref[pl.ds(i0, B), c0:c0 + CW] -= jnp.dot(lhs, ur_ref[:, c0:c0 + CW], preferred_element_type=f32)

            update(N)
            update(CW)

            @pl.when(i < NB // 2)
            def _():
                update(0)

    var = var_ref[...] * (4.0 / P_SIZE)
    moder = jnp.exp(logits / jnp.sqrt(1.0 + var))
    moder = moder / jnp.sum(moder, axis=0, keepdims=True)
    mod_ref[0:C, :] = moder

    def member_copy(rel):
        return pltpu.make_async_remote_copy(
            src_ref=mod_ref, dst_ref=got_ref.at[rel - 1], send_sem=es_sem, recv_sem=er_sem,
            device_id=(members[rel - 1], d), device_id_type=MESH)

    for rel in range(1, MEMBERS):
        member_copy(rel).start()
    for g in range(len(GROUPS)):
        mate_copy(g).wait_send()
        part_all(g).wait_send()
        row_all(g).wait_send()
        forward_copy(g).wait_send()
    every = pltpu.make_async_remote_copy(
        src_ref=got_ref, dst_ref=got_ref, send_sem=es_sem, recv_sem=er_sem, device_id=(m, to_m), device_id_type=MESH)
    every.wait_recv()
    total = moder
    for rel in range(1, MEMBERS):
        total += got_ref[rel - 1, 0:C, :]
    out_ref[0:C, :] = total * f32(1.0 / MEMBERS)
    out_ref[C:C + 1, :] = var
    every.wait_send()
    for cp in sends:
        cp.wait_send()


def laplace(hidden, proj, hw, hb, prior, labels, cw):
    vm = pl.BlockSpec(memory_space=pltpu.VMEM)
    any_ = pl.BlockSpec(memory_space=pl.ANY)
    dma = pltpu.SemaphoreType.DMA
    return pl.pallas_call(
        laplace_kernel,
        out_shape=jax.ShapeDtypeStruct((16, R_), f32),
        in_specs=[any_, any_, vm, vm, vm, vm, vm],
        out_specs=vm,
        scratch_shapes=[
            pltpu.VMEM((R_, 4096), bf16),
            pltpu.VMEM((8, 2 * KB, P_SIZE), bf16),
            pltpu.VMEM((R_, P_SIZE), f32),
            pltpu.VMEM((N, R_), bf16),
            pltpu.VMEM((N, R_), bf16),
            pltpu.VMEM((NB, B, N), f32),
            pltpu.VMEM((NB, B // 2, N), f32),
            pltpu.VMEM((NB, 56, N), f32),
            pltpu.VMEM((NB, B, N), f32),
            pltpu.VMEM((1, R_), f32),
            pltpu.VMEM((N, W), f32),
            pltpu.VMEM((B, B), f32),
            pltpu.VMEM((N, 3 * B), bf16),
            pltpu.VMEM((3 * B, W), bf16),
            pltpu.VMEM((16, R_), f32),
            pltpu.VMEM((MEMBERS - 1, 16, R_), f32),
            dma((2,)), dma((30,)), dma((16, 2)),
            dma((5,)), dma((5,)), dma((5,)), dma((5,)), dma((5,)), dma((5,)), dma((5,)), dma((5,)),
            dma, dma,
        ],
        compiler_params=pltpu.CompilerParams(
            collective_id=0, has_side_effects=True, vmem_limit_bytes=56 * 1024 * 1024),
    )(hidden, proj, hw, hb, prior, labels, cw)


def finish_kernel(pack_ref, var_ref, ens_ref):
    ens_ref[...] = pack_ref[0:C, :]
    var_ref[...] = pack_ref[C:C + 1, :]


def body(hidden, projection, head_weight, head_bias, prior_precision, labels, category_weight):
    pack = laplace(
        hidden[0], projection[0], head_weight[0], head_bias, prior_precision, labels[None, :], category_weight[None, :])
    vm = pl.BlockSpec(memory_space=pltpu.VMEM)
    return pl.pallas_call(
        finish_kernel,
        out_shape=(jax.ShapeDtypeStruct((1, R_), f32), jax.ShapeDtypeStruct((C, R_), f32)),
        in_specs=[vm],
        out_specs=(vm, vm),
    )(pack)


def solution(mesh):
    return jax.shard_map(
        body,
        mesh=mesh,
        in_specs=(
            P("member", "dp", None),
            P("member", "dp", None),
            P("member", None, None),
            P("member", None),
            P("member", None),
            P("dp"),
            P(),
        ),
        out_specs=(P("member", "dp"), P(None, "dp")),
        check_vma=False,
    )
```

```python
import jax, jax.numpy as jnp
from jax import lax
from jax.experimental import pallas as pl
from jax.experimental.pallas import tpu as pltpu
from jax.sharding import PartitionSpec as P

N = 1024
P_SIZE = 1024
ROWS = 8192
B = 128
NB = N // B
R_ = 512
W = N + R_
f32 = jnp.float32
bf16 = jnp.bfloat16


def split3(x):
    hi = x.astype(bf16)
    lo = (x - hi.astype(f32)).astype(bf16)
    return hi, lo


SB = 4
NEXT = 2


def diag_inverse(S, hook=lambda b: None):
    G = 8
    n = B // G
    T = list(S)
    lane = lax.broadcasted_iota(jnp.int32, (G, B), 1)
    sub = lax.broadcasted_iota(jnp.int32, (G, B), 0)
    out = [None] * n
    held = []

    def column(t, j):
        return jnp.take_along_axis(t, jnp.full((G, B), j, jnp.int32), axis=1)

    def row(t, j):
        return jnp.broadcast_to(t[j:j + 1, :], (G, B))

    for b in range(n):
        hook(b)
        first = b - b % SB
        edge = min(first + SB + NEXT, n)
        cb = [column(T[b], G * b + k) for k in range(G)]
        below = range(b + 1, edge)
        cn = {i: [column(T[i], G * b + k) for k in range(G)] for i in below}
        own = (lane >= G * b) & (lane < G * b + G)
        tn = {i: jnp.where(own, f32(0), T[i]) for i in below}
        rb = T[b]
        qb = jnp.where(lane < G * b, rb, jnp.where(lane == sub + G * b, f32(1), f32(0)))
        dv = jnp.ones((G, B), f32)
        iv = jnp.ones((G, B), f32)
        for j in range(G):
            p = row(cb[j], j)
            inv = 1.0 / p
            dv = jnp.where(sub == j, p, dv)
            iv = jnp.where(sub == j, inv, iv)
            m = jnp.where(sub > j, cb[j] * inv, f32(0))
            mn = {i: cn[i][j] * inv for i in below}
            for k in range(j + 1, G):
                r = row(cb[k], j)
                cb[k] = cb[k] - m * r
                for i in below:
                    cn[i][k] = cn[i][k] - mn[i] * r
            q = row(qb, j)
            if b < n - 1:
                r = row(rb, j)
                full = jnp.where(lane < G * b + G, q, r)
                for i in below:
                    tn[i] = tn[i] - mn[i] * full
                if j < G - 1:
                    rb = rb - m * r
            if j < G - 1:
                qb = qb - m * q
        out[b] = qb * lax.rsqrt(dv)
        for i in below:
            T[i] = tn[i]
        if edge < n:
            end = G * (first + SB)
            held.append((rb * iv, jnp.where(lane < G * b + G, qb, jnp.where(lane < end, f32(0), rb))))
            if b == first + SB - 1:
                left = jnp.concatenate([x for x, _ in held], axis=0)
                right = jnp.concatenate([y for _, y in held], axis=0)
                lh, ll = split3(left)
                rh, rl = split3(right)
                prod = lax.dot_general(
                    jnp.concatenate([lh, lh, ll], axis=0), jnp.concatenate([rh, rl, rh], axis=0),
                    (((0,), (0,)), ((), ())), preferred_element_type=f32)
                region = (lane >= G * first) & (lane < end)
                for i in range(edge, n):
                    T[i] = jnp.where(region, f32(0), T[i]) - prod[G * i:G * i + G, :]
                held = []
    return out


MESH = pl.DeviceIdType.MESH
C = 14
MEMBERS = 8
GROUPS = (
    (0, 1, 0, 128),
    (0, 1, 128, 896),
    (1, 1, 128, 128),
    (1, 1, 256, 768),
    (2, 1, 256, 128),
    (2, 1, 384, 640),
    (3, 1, 384, 128),
    (3, 1, 512, 512),
    (4, 1, 512, 512),
    (5, 1, 640, 384),
    (6, 2, 768, 256),
)
KB = 256
SLAB = 6 * B
MN = 512


def laplace_kernel(hid_ref, proj_ref, hw_ref, hb_ref, prior_ref, lab_ref, cw_ref, out_ref,
                   h_ref, buf_ref, acc_ref, ft_ref, wt_ref, gp_ref, mate_ref, part_ref, a_ref, var_ref,
                   g_ref, linv_ref, ul_ref, ur_ref, mod_ref, got_ref,
                   loc_sem, send_sem, recv_sem, ms_sem, mr_sem, ss_sem, sr_sem, gs_sem, gr_sem, fs_sem, fr_sem,
                   es_sem, er_sem):
    m = lax.axis_index("member")
    d = lax.axis_index("dp")
    c = lax.rem(d, 2)
    x = lax.rem(d // 2, 4)
    yh = d // 8

    def dp(dy, dx, t):
        yy = yh if dy == 0 else 1 - yh
        cc = c if t == 0 else 1 - c
        return (yy * 4 + lax.rem(x + dx, 4)) * 2 + cc

    to_r, to_l, to_y, to_m = dp(0, 1, 0), dp(0, 3, 0), dp(1, 0, 0), dp(0, 0, 1)
    me = d
    own_copy = pltpu.make_async_copy(proj_ref, buf_ref.at[d // 2, pl.ds(pl.multiple_of(c * KB, KB), KB), :], loc_sem.at[0])
    own_copy.start()
    hid_copy = pltpu.make_async_copy(hid_ref, h_ref, loc_sem.at[1])
    hid_copy.start()
    bar = pltpu.get_barrier_semaphore()
    chip = d // 2
    peers = [lax.rem(chip + rel, 8) * 2 + c for rel in range(1, 8)]
    for t in peers + [to_m]:
        pl.semaphore_signal(bar, inc=1, device_id=(m, t), device_id_type=MESH)
    members = [lax.rem(m + rel, MEMBERS) for rel in range(1, MEMBERS)]
    for t in members:
        pl.semaphore_signal(bar, inc=1, device_id=(t, d), device_id_type=MESH)
    pl.semaphore_wait(bar, 15)
    own_copy.wait()
    sends = []

    def half(s, h):
        return buf_ref.at[s // 2, pl.ds(pl.multiple_of(lax.rem(s, 2) * KB + h * (KB // 2), KB // 2), KB // 2), :]

    def copy(s, h, to, i):
        return pltpu.make_async_remote_copy(
            src_ref=half(s, h), dst_ref=half(s, h), send_sem=send_sem.at[i], recv_sem=recv_sem.at[s, h],
            device_id=(m, to), device_id_type=MESH)

    def send(to, s, h):
        cp = copy(s, h, to, len(sends))
        cp.start()
        sends.append(cp)

    def wait(s, h):
        copy(s, h, to_m, 0).wait_recv()

    def mm(s, first=False):
        place = s // 2
        k0 = pl.multiple_of(place * 2 * KB, 2 * KB)

        @pl.loop(0, P_SIZE // MN)
        def _(n):
            n0 = pl.multiple_of(n * MN, MN)
            r = jnp.dot(h_ref[:, pl.ds(k0, 2 * KB)], buf_ref[place, :, pl.ds(n0, MN)], preferred_element_type=f32)
            if first:
                acc_ref[:, pl.ds(n0, MN)] = r
            else:
                acc_ref[:, pl.ds(n0, MN)] += r

    left, right, anti, part = dp(0, 3, 0), dp(0, 1, 0), dp(0, 2, 0), dp(1, 0, 0)
    far_l, far_r, far_a = dp(1, 3, 0), dp(1, 1, 0), dp(1, 2, 0)

    def mate_mm(dy, dx, first=False):
        s = dp(dy, dx, 1)
        wait(s, 0)
        wait(s, 1)
        mm(s, first)

    send(to_r, me, 0)
    send(to_l, me, 1)
    send(to_y, me, 0)
    send(to_y, me, 1)
    send(to_r, me, 1)
    send(to_l, me, 0)
    send(to_m, me, 0)
    send(to_m, me, 1)
    for i in range(NB):
        g_ref[B * i:B * (i + 1), :N] = jnp.zeros((B, N), f32)
    hid_copy.wait()
    wait(left, 0)
    send(to_r, left, 0)
    send(to_y, left, 0)
    wait(right, 1)
    send(to_l, right, 1)
    send(to_y, right, 1)
    send(to_m, left, 0)
    send(to_m, right, 1)
    wait(part, 0)
    send(to_l, part, 0)
    wait(part, 1)
    send(to_r, part, 1)
    send(to_m, part, 0)
    send(to_m, part, 1)
    wait(left, 1)
    send(to_m, left, 1)
    wait(right, 0)
    send(to_m, right, 0)
    mate_mm(0, 0, True)
    mate_mm(0, 3)
    mate_mm(0, 1)
    wait(anti, 0)
    send(to_m, anti, 0)
    wait(anti, 1)
    send(to_m, anti, 1)
    wait(far_l, 0)
    send(to_r, far_l, 0)
    wait(far_r, 1)
    send(to_l, far_r, 1)
    send(to_m, far_l, 0)
    send(to_m, far_r, 1)
    mate_mm(1, 0)
    mate_mm(0, 2)
    wait(far_l, 1)
    send(to_m, far_l, 1)
    wait(far_r, 0)
    send(to_m, far_r, 0)
    mate_mm(1, 3)
    mate_mm(1, 1)
    wait(far_a, 0)
    send(to_m, far_a, 0)
    wait(far_a, 1)
    send(to_m, far_a, 1)
    mate_mm(1, 2)

    for j in range(NB):
        ft_ref[B * j:B * (j + 1), :] = acc_ref[:, B * j:B * (j + 1)].T.astype(bf16)
    eye = lax.broadcasted_iota(jnp.int32, (C, C), 0) == lax.broadcasted_iota(jnp.int32, (C, C), 1)
    bias = jnp.sum(jnp.where(eye, hb_ref[...], f32(0)), axis=1, keepdims=True)
    weight = jnp.sum(jnp.where(eye, cw_ref[...].astype(f32), f32(0)), axis=1, keepdims=True)
    logits = jnp.dot(hw_ref[...], ft_ref[...], preferred_element_type=f32) + bias
    cat = lax.broadcasted_iota(jnp.int32, (C, R_), 0)
    row_weight = jnp.sum(jnp.where(cat == lab_ref[...], weight, f32(0)), axis=0, keepdims=True)
    expo = jnp.exp(logits)
    probs = expo / jnp.sum(expo, axis=0, keepdims=True)
    curv = row_weight * (1.0 - jnp.sum(probs * probs, axis=0, keepdims=True))
    root = jnp.sqrt(curv)
    for j in range(NB):
        wt_ref[B * j:B * (j + 1), :] = (ft_ref[B * j:B * (j + 1), :].astype(f32) * root).astype(bf16)

    H = B // 2
    mine = pl.multiple_of(c * H, H)
    other = pl.multiple_of((1 - c) * H, H)
    slice_at = pl.multiple_of(mine + 8 * chip, 8)

    def remote(src, dst, sems, g, to):
        return pltpu.make_async_remote_copy(
            src_ref=src, dst_ref=dst, send_sem=sems[0].at[g], recv_sem=sems[1].at[g], device_id=(m, to), device_id_type=MESH)

    def view(ref, g, row0, rows):
        p0, count, col0, width = GROUPS[g]
        return ref.at[pl.ds(p0, count), pl.ds(row0, rows), pl.ds(col0, width)]

    def mate_copy(g):
        return remote(view(gp_ref, g, other, H), view(mate_ref, g, 0, H), (ms_sem, mr_sem), g, to_m)

    def part_copy(g, rel):
        to = lax.rem(chip + rel, 8)
        return remote(view(gp_ref, g, pl.multiple_of(mine + 8 * to, 8), 8), view(part_ref, g, 8 * (rel - 1), 8),
                      (ss_sem, sr_sem), g, to * 2 + c)

    def part_all(g):
        return remote(view(part_ref, g, 0, 56), view(part_ref, g, 0, 56), (ss_sem, sr_sem), g, to_m)

    def row_copy(g, rel):
        ref = view(a_ref, g, slice_at, 8)
        return remote(ref, ref, (gs_sem, gr_sem), g, lax.rem(chip + rel, 8) * 2 + c)

    def row_all(g):
        ref = view(a_ref, g, mine, 56)
        return remote(ref, ref, (gs_sem, gr_sem), g, to_m)

    def forward_copy(g):
        ref = view(a_ref, g, mine, H)
        return remote(ref, ref, (fs_sem, fr_sem), g, to_m)

    def scatter(g):
        p0, count, col0, width = GROUPS[g]
        mate_copy(g).wait_recv()
        for p in range(p0, p0 + count):
            gp_ref[p, pl.ds(mine, H), col0:col0 + width] += mate_ref[p, :, col0:col0 + width]
        for rel in range(1, 8):
            part_copy(g, rel).start()

    def reduce(g):
        p0, count, col0, width = GROUPS[g]
        part_all(g).wait_recv()
        for p in range(p0, p0 + count):
            total = gp_ref[p, pl.ds(slice_at, 8), col0:col0 + width]
            for rel in range(1, 8):
                total += part_ref[p, 8 * (rel - 1):8 * rel, col0:col0 + width]
            a_ref[p, pl.ds(slice_at, 8), col0:col0 + width] = total
        for rel in range(1, 8):
            row_copy(g, rel).start()

    def forward(g):
        row_all(g).wait_recv()
        forward_copy(g).start()

    for g, (p0, count, col0, width) in enumerate(GROUPS):
        for p in range(p0, p0 + count):
            gp_ref[p, :, col0:col0 + width] = lax.dot_general(
                wt_ref[B * p:B * (p + 1), :], wt_ref[col0:col0 + width, :], (((1,), (1,)), ((), ())), preferred_element_type=f32)
        mate_copy(g).start()
        if g == 1:
            scatter(0)
    done = lambda g: forward_copy(g).wait_recv()
    scatter(1)
    reduce(0)
    for i in range(NB):
        g_ref[B * i:B * (i + 1), N:] = ft_ref[B * i:B * (i + 1), :].astype(f32)
    var_ref[...] = jnp.zeros_like(var_ref)
    ul_ref[...] = jnp.zeros_like(ul_ref)
    ur_ref[...] = jnp.zeros_like(ur_ref)
    scatter(2)
    scatter(3)
    forward(0)
    reduce(1)
    done(0)
    at_start = {1: [(forward, 1)], 2: [(scatter, 10)], 3: [(reduce, 10)]}
    before_rows = {1: [(done, 1), (forward, 2), (reduce, 4), (scatter, 6), (reduce, 5)], 2: [(done, 3)], 3: [(done, 5)], 4: [(done, 7)]}
    before_block = {0: [(reduce, 2)], 1: [(done, 2), (scatter, 7)], 2: [(done, 4), (reduce, 7), (forward, 6)], 3: [(done, 6)], 4: [(done, 8), (forward, 10)], 5: [(done, 9)], 6: [(done, 10)]}
    middle = {
        2: {3: [(forward, 7)]},
        5: {0: [(scatter, 4), (scatter, 5), (reduce, 3)], 1: [(forward, 3)]},
        8: {1: [(forward, 4), (reduce, 6), (scatter, 8)], 2: [(reduce, 8)], 3: [(forward, 8)]},
        11: {2: [(reduce, 9)]},
        14: {1: [(scatter, 9), (forward, 5)], 3: [(forward, 9)]},
    }

    def run(table, k):
        for key, steps in table.items():
            @pl.when(k == key)
            def _(steps=steps):
                for step, g in steps:
                    step(g)

    diag_r = lax.broadcasted_iota(jnp.int32, (8, B), 0)
    diag_c = lax.broadcasted_iota(jnp.int32, (8, B), 1)
    CW = 512

    def row_panel(p, c0, with_a, lcat):
        g = g_ref[pl.ds(pl.multiple_of(p * B, B), B), c0:c0 + CW]
        if with_a:
            g = g + a_ref[p, :, c0:c0 + CW] * f32(1.0 / ROWS)
        gh, gl = split3(g)
        u = jnp.dot(lcat, jnp.concatenate([gh, gh, gl], axis=0), preferred_element_type=f32)
        uh, ul = split3(u)
        ur_ref[0:B, c0:c0 + CW] = uh
        ur_ref[B:2 * B, c0:c0 + CW] = uh
        ur_ref[2 * B:, c0:c0 + CW] = ul
        if with_a:
            for t in range(CW // B):
                th, tl = split3(u[:, B * t:B * (t + 1)].T)
                r0 = c0 + B * t
                ul_ref[r0:r0 + B, 0:B] = th
                ul_ref[r0:r0 + B, B:2 * B] = tl
                ul_ref[r0:r0 + B, 2 * B:] = th
        else:
            var_ref[...] += jnp.sum(u * u, axis=0, keepdims=True)

    def inverse_factor():
        lh, ll = split3(linv_ref[...])
        return jnp.concatenate([lh, ll, lh], axis=1)

    @pl.loop(0, NB)
    def _(k):
        k0 = pl.multiple_of(k * B, B)
        run(at_start, k)

        @pl.when(k > 0)
        def _():
            lcat = inverse_factor()
            row_panel(k - 1, N, False, lcat)
            run(before_rows, k)
            row_panel(k - 1, CW, True, lcat)

            @pl.when(k < NB // 2)
            def _():
                row_panel(k - 1, 0, True, lcat)
            lhs = ul_ref[pl.ds(k0, B), :]
            for c0 in (CW, N):
                g_ref[pl.ds(k0, B), c0:c0 + CW] -= jnp.dot(lhs, ur_ref[:, c0:c0 + CW], preferred_element_type=f32)

            @pl.when(k < NB // 2)
            def _():
                g_ref[pl.ds(k0, B), 0:CW] -= jnp.dot(lhs, ur_ref[:, 0:CW], preferred_element_type=f32)
        run(before_block, k)
        pr = prior_ref[:, pl.ds(k0, B)]
        S = []
        for i in range(16):
            s = g_ref[pl.ds(k0 + 8 * i, 8), pl.ds(k0, B)] + a_ref[k, pl.ds(8 * i, 8), pl.ds(k0, B)] * f32(1.0 / ROWS)
            S.append(s + jnp.where(diag_c == diag_r + 8 * i, pr, f32(0)))
        rows = pl.ds(pl.multiple_of(k0 + B, B), SLAB)

        def hook(b):
            if b in middle:
                run(middle[b], k)
            if b % 2 == 1 and b // 2 < W // 256:
                cols = slice(b // 2 * 256, (b // 2 + 1) * 256)
                g_ref[rows, cols] -= jnp.dot(ul_ref[rows, :], ur_ref[:, cols], preferred_element_type=f32)
        out = diag_inverse(S, hook)
        for i in range(16):
            linv_ref[pl.ds(8 * i, 8), :] = out[i]

    row_panel(NB - 1, N, False, inverse_factor())
    var = var_ref[...] * (4.0 / P_SIZE)
    moder = jnp.exp(logits / jnp.sqrt(1.0 + var))
    moder = moder / jnp.sum(moder, axis=0, keepdims=True)
    mod_ref[0:C, :] = moder

    def member_copy(rel):
        return pltpu.make_async_remote_copy(
            src_ref=mod_ref, dst_ref=got_ref.at[rel - 1], send_sem=es_sem, recv_sem=er_sem,
            device_id=(members[rel - 1], d), device_id_type=MESH)

    for rel in range(1, MEMBERS):
        member_copy(rel).start()
    for g in range(len(GROUPS)):
        mate_copy(g).wait_send()
        part_all(g).wait_send()
        row_all(g).wait_send()
        forward_copy(g).wait_send()
    every = pltpu.make_async_remote_copy(
        src_ref=got_ref, dst_ref=got_ref, send_sem=es_sem, recv_sem=er_sem, device_id=(m, to_m), device_id_type=MESH)
    every.wait_recv()
    total = moder
    for rel in range(1, MEMBERS):
        total += got_ref[rel - 1, 0:C, :]
    out_ref[0:C, :] = total * f32(1.0 / MEMBERS)
    out_ref[C:C + 1, :] = var
    every.wait_send()
    for cp in sends:
        cp.wait_send()


def laplace(hidden, proj, hw, hb, prior, labels, cw):
    vm = pl.BlockSpec(memory_space=pltpu.VMEM)
    any_ = pl.BlockSpec(memory_space=pl.ANY)
    dma = pltpu.SemaphoreType.DMA
    return pl.pallas_call(
        laplace_kernel,
        out_shape=jax.ShapeDtypeStruct((16, R_), f32),
        in_specs=[any_, any_, vm, vm, vm, vm, vm],
        out_specs=vm,
        scratch_shapes=[
            pltpu.VMEM((R_, 4096), bf16),
            pltpu.VMEM((8, 2 * KB, P_SIZE), bf16),
            pltpu.VMEM((R_, P_SIZE), f32),
            pltpu.VMEM((N, R_), bf16),
            pltpu.VMEM((N, R_), bf16),
            pltpu.VMEM((NB, B, N), f32),
            pltpu.VMEM((NB, B // 2, N), f32),
            pltpu.VMEM((NB, 56, N), f32),
            pltpu.VMEM((NB, B, N), f32),
            pltpu.VMEM((1, R_), f32),
            pltpu.VMEM((N + SLAB, W), f32),
            pltpu.VMEM((B, B), f32),
            pltpu.VMEM((N + SLAB, 3 * B), bf16),
            pltpu.VMEM((3 * B, W), bf16),
            pltpu.VMEM((16, R_), f32),
            pltpu.VMEM((MEMBERS - 1, 16, R_), f32),
            dma((2,)), dma((30,)), dma((16, 2)),
            dma((11,)), dma((11,)), dma((11,)), dma((11,)), dma((11,)), dma((11,)), dma((11,)), dma((11,)),
            dma, dma,
        ],
        compiler_params=pltpu.CompilerParams(
            collective_id=0, has_side_effects=True, vmem_limit_bytes=56 * 1024 * 1024),
    )(hidden, proj, hw, hb, prior, labels, cw)


def finish_kernel(pack_ref, var_ref, ens_ref):
    ens_ref[...] = pack_ref[0:C, :]
    var_ref[...] = pack_ref[C:C + 1, :]


def body(hidden, projection, head_weight, head_bias, prior_precision, labels, category_weight):
    pack = laplace(
        hidden[0], projection[0], head_weight[0], head_bias, prior_precision, labels[None, :], category_weight[None, :])
    vm = pl.BlockSpec(memory_space=pltpu.VMEM)
    return pl.pallas_call(
        finish_kernel,
        out_shape=(jax.ShapeDtypeStruct((1, R_), f32), jax.ShapeDtypeStruct((C, R_), f32)),
        in_specs=[vm],
        out_specs=(vm, vm),
    )(pack)


def solution(mesh):
    return jax.shard_map(
        body,
        mesh=mesh,
        in_specs=(
            P("member", "dp", None),
            P("member", "dp", None),
            P("member", None, None),
            P("member", None),
            P("member", None),
            P("dp"),
            P(),
        ),
        out_specs=(P("member", "dp"), P(None, "dp")),
        check_vma=False,
    )
```

```python
import jax, jax.numpy as jnp
from jax import lax
from jax.experimental import pallas as pl
from jax.experimental.pallas import tpu as pltpu
from jax.sharding import PartitionSpec as P

N = 1024
P_SIZE = 1024
ROWS = 8192
B = 128
NB = N // B
R_ = 512
W = N + R_
f32 = jnp.float32
bf16 = jnp.bfloat16


def split3(x):
    hi = x.astype(bf16)
    lo = (x - hi.astype(f32)).astype(bf16)
    return hi, lo


SB = 4
NEXT = 1


def diag_inverse(S, hook=lambda b: None):
    G = 8
    n = B // G
    T = list(S)
    lane = lax.broadcasted_iota(jnp.int32, (G, B), 1)
    sub = lax.broadcasted_iota(jnp.int32, (G, B), 0)
    out = [None] * n
    held = []

    def column(t, j):
        return jnp.take_along_axis(t, jnp.full((G, B), j, jnp.int32), axis=1)

    def row(t, j):
        return jnp.broadcast_to(t[j:j + 1, :], (G, B))

    for b in range(n):
        hook(b)
        first = b - b % SB
        edge = min(first + SB + NEXT, n)
        cb = ahead if b else [column(T[b], G * b + k) for k in range(G)]
        below = range(b + 1, edge)
        cn = {i: [column(T[i], G * b + k) for k in range(G)] for i in below}
        if b < n - 1:
            ahead = [column(T[b + 1], G * (b + 1) + k) for k in range(G)]
        own = (lane >= G * b) & (lane < G * b + G)
        tn = {i: jnp.where(own, f32(0), T[i]) for i in below}
        rb = T[b]
        qb = jnp.where(lane < G * b, rb, jnp.where(lane == sub + G * b, f32(1), f32(0)))
        dv = jnp.ones((G, B), f32)
        iv = jnp.ones((G, B), f32)
        for j in range(G):
            p = row(cb[j], j)
            inv = 1.0 / p
            dv = jnp.where(sub == j, p, dv)
            iv = jnp.where(sub == j, inv, iv)
            m = jnp.where(sub > j, cb[j] * inv, f32(0))
            mn = {i: cn[i][j] * inv for i in below}
            if b < n - 1:
                for k in range(G):
                    ahead[k] = ahead[k] - mn[b + 1] * row(cn[b + 1][j], k)
            for k in range(j + 1, G):
                r = row(cb[k], j)
                cb[k] = cb[k] - m * r
                for i in below:
                    cn[i][k] = cn[i][k] - mn[i] * r
            q = row(qb, j)
            if b < n - 1:
                r = row(rb, j)
                full = jnp.where(lane < G * b + G, q, r)
                for i in below:
                    tn[i] = tn[i] - mn[i] * full
                if j < G - 1:
                    rb = rb - m * r
            if j < G - 1:
                qb = qb - m * q
        out[b] = qb * lax.rsqrt(dv)
        for i in below:
            T[i] = tn[i]
        if edge < n:
            end = G * (first + SB)
            held.append((rb * iv, jnp.where(lane < G * b + G, qb, jnp.where(lane < end, f32(0), rb))))
            if b == first + SB - 1:
                left = jnp.concatenate([x for x, _ in held], axis=0)
                right = jnp.concatenate([y for _, y in held], axis=0)
                lh, ll = split3(left)
                rh, rl = split3(right)
                prod = lax.dot_general(
                    jnp.concatenate([lh, lh, ll], axis=0), jnp.concatenate([rh, rl, rh], axis=0),
                    (((0,), (0,)), ((), ())), preferred_element_type=f32)
                region = (lane >= G * first) & (lane < end)
                for i in range(edge, n):
                    T[i] = jnp.where(region, f32(0), T[i]) - prod[G * i:G * i + G, :]
                held = []
    return out


MESH = pl.DeviceIdType.MESH
C = 14
MEMBERS = 8
GROUPS = (
    (0, 1, 0, 128),
    (0, 1, 128, 896),
    (1, 1, 128, 128),
    (1, 1, 256, 768),
    (2, 1, 256, 768),
    (3, 1, 384, 640),
    (4, 2, 512, 512),
    (6, 2, 768, 256),
)
KB = 256
SLAB = 6 * B
MN = 512


def laplace_kernel(hid_ref, proj_ref, hw_ref, hb_ref, prior_ref, lab_ref, cw_ref, out_ref,
                   h_ref, buf_ref, acc_ref, ft_ref, wt_ref, gp_ref, mate_ref, part_ref, a_ref, var_ref,
                   g_ref, linv_ref, ul_ref, ur_ref, mod_ref, got_ref,
                   loc_sem, send_sem, recv_sem, ms_sem, mr_sem, ss_sem, sr_sem, gs_sem, gr_sem, fs_sem, fr_sem,
                   es_sem, er_sem):
    m = lax.axis_index("member")
    d = lax.axis_index("dp")
    c = lax.rem(d, 2)
    x = lax.rem(d // 2, 4)
    yh = d // 8

    def dp(dy, dx, t):
        yy = yh if dy == 0 else 1 - yh
        cc = c if t == 0 else 1 - c
        return (yy * 4 + lax.rem(x + dx, 4)) * 2 + cc

    to_r, to_l, to_y, to_m = dp(0, 1, 0), dp(0, 3, 0), dp(1, 0, 0), dp(0, 0, 1)
    me = d
    own_copy = pltpu.make_async_copy(proj_ref, buf_ref.at[d // 2, pl.ds(pl.multiple_of(c * KB, KB), KB), :], loc_sem.at[0])
    own_copy.start()
    hid_copy = pltpu.make_async_copy(hid_ref, h_ref, loc_sem.at[1])
    hid_copy.start()
    bar = pltpu.get_barrier_semaphore()
    chip = d // 2
    peers = [lax.rem(chip + rel, 8) * 2 + c for rel in range(1, 8)]
    for t in peers + [to_m]:
        pl.semaphore_signal(bar, inc=1, device_id=(m, t), device_id_type=MESH)
    members = [lax.rem(m + rel, MEMBERS) for rel in range(1, MEMBERS)]
    for t in members:
        pl.semaphore_signal(bar, inc=1, device_id=(t, d), device_id_type=MESH)
    pl.semaphore_wait(bar, 15)
    own_copy.wait()
    sends = []

    def half(s, h):
        return buf_ref.at[s // 2, pl.ds(pl.multiple_of(lax.rem(s, 2) * KB + h * (KB // 2), KB // 2), KB // 2), :]

    def copy(s, h, to, i):
        return pltpu.make_async_remote_copy(
            src_ref=half(s, h), dst_ref=half(s, h), send_sem=send_sem.at[i], recv_sem=recv_sem.at[s, h],
            device_id=(m, to), device_id_type=MESH)

    def send(to, s, h):
        cp = copy(s, h, to, len(sends))
        cp.start()
        sends.append(cp)

    def wait(s, h):
        copy(s, h, to_m, 0).wait_recv()

    def mm(s, first=False):
        place = s // 2
        k0 = pl.multiple_of(place * 2 * KB, 2 * KB)

        @pl.loop(0, P_SIZE // MN)
        def _(n):
            n0 = pl.multiple_of(n * MN, MN)
            r = jnp.dot(h_ref[:, pl.ds(k0, 2 * KB)], buf_ref[place, :, pl.ds(n0, MN)], preferred_element_type=f32)
            if first:
                acc_ref[:, pl.ds(n0, MN)] = r
            else:
                acc_ref[:, pl.ds(n0, MN)] += r

    left, right, anti, part = dp(0, 3, 0), dp(0, 1, 0), dp(0, 2, 0), dp(1, 0, 0)
    far_l, far_r, far_a = dp(1, 3, 0), dp(1, 1, 0), dp(1, 2, 0)

    def mate_mm(dy, dx, first=False):
        s = dp(dy, dx, 1)
        wait(s, 0)
        wait(s, 1)
        mm(s, first)

    send(to_r, me, 0)
    send(to_l, me, 1)
    send(to_y, me, 0)
    send(to_y, me, 1)
    send(to_r, me, 1)
    send(to_l, me, 0)
    send(to_m, me, 0)
    send(to_m, me, 1)
    for i in range(NB):
        g_ref[B * i:B * (i + 1), :N] = jnp.zeros((B, N), f32)
    hid_copy.wait()
    wait(left, 0)
    send(to_r, left, 0)
    send(to_y, left, 0)
    wait(right, 1)
    send(to_l, right, 1)
    send(to_y, right, 1)
    send(to_m, left, 0)
    send(to_m, right, 1)
    wait(part, 0)
    send(to_l, part, 0)
    wait(part, 1)
    send(to_r, part, 1)
    send(to_m, part, 0)
    send(to_m, part, 1)
    wait(left, 1)
    send(to_m, left, 1)
    wait(right, 0)
    send(to_m, right, 0)
    mate_mm(0, 0, True)
    mate_mm(0, 3)
    mate_mm(0, 1)
    wait(anti, 0)
    send(to_m, anti, 0)
    wait(anti, 1)
    send(to_m, anti, 1)
    wait(far_l, 0)
    send(to_r, far_l, 0)
    wait(far_r, 1)
    send(to_l, far_r, 1)
    send(to_m, far_l, 0)
    send(to_m, far_r, 1)
    mate_mm(1, 0)
    mate_mm(0, 2)
    wait(far_l, 1)
    send(to_m, far_l, 1)
    wait(far_r, 0)
    send(to_m, far_r, 0)
    mate_mm(1, 3)
    mate_mm(1, 1)
    wait(far_a, 0)
    send(to_m, far_a, 0)
    wait(far_a, 1)
    send(to_m, far_a, 1)
    mate_mm(1, 2)

    for j in range(NB):
        ft_ref[B * j:B * (j + 1), :] = acc_ref[:, B * j:B * (j + 1)].T.astype(bf16)
    eye = lax.broadcasted_iota(jnp.int32, (C, C), 0) == lax.broadcasted_iota(jnp.int32, (C, C), 1)
    bias = jnp.sum(jnp.where(eye, hb_ref[...], f32(0)), axis=1, keepdims=True)
    weight = jnp.sum(jnp.where(eye, cw_ref[...].astype(f32), f32(0)), axis=1, keepdims=True)
    logits = jnp.dot(hw_ref[...], ft_ref[...], preferred_element_type=f32) + bias
    cat = lax.broadcasted_iota(jnp.int32, (C, R_), 0)
    row_weight = jnp.sum(jnp.where(cat == lab_ref[...], weight, f32(0)), axis=0, keepdims=True)
    expo = jnp.exp(logits)
    probs = expo / jnp.sum(expo, axis=0, keepdims=True)
    curv = row_weight * (1.0 - jnp.sum(probs * probs, axis=0, keepdims=True))
    root = jnp.sqrt(curv)
    for j in range(NB):
        wt_ref[B * j:B * (j + 1), :] = (ft_ref[B * j:B * (j + 1), :].astype(f32) * root).astype(bf16)

    H = B // 2
    mine = pl.multiple_of(c * H, H)
    other = pl.multiple_of((1 - c) * H, H)
    slice_at = pl.multiple_of(mine + 8 * chip, 8)

    def remote(src, dst, sems, g, to):
        return pltpu.make_async_remote_copy(
            src_ref=src, dst_ref=dst, send_sem=sems[0].at[g], recv_sem=sems[1].at[g], device_id=(m, to), device_id_type=MESH)

    def view(ref, g, row0, rows):
        p0, count, col0, width = GROUPS[g]
        return ref.at[pl.ds(p0, count), pl.ds(row0, rows), pl.ds(col0, width)]

    def mate_copy(g):
        return remote(view(gp_ref, g, other, H), view(mate_ref, g, 0, H), (ms_sem, mr_sem), g, to_m)

    def part_copy(g, rel):
        to = lax.rem(chip + rel, 8)
        return remote(view(gp_ref, g, pl.multiple_of(mine + 8 * to, 8), 8), view(part_ref, g, 8 * (rel - 1), 8),
                      (ss_sem, sr_sem), g, to * 2 + c)

    def part_all(g):
        return remote(view(part_ref, g, 0, 56), view(part_ref, g, 0, 56), (ss_sem, sr_sem), g, to_m)

    def row_copy(g, rel):
        ref = view(a_ref, g, slice_at, 8)
        return remote(ref, ref, (gs_sem, gr_sem), g, lax.rem(chip + rel, 8) * 2 + c)

    def row_all(g):
        ref = view(a_ref, g, mine, 56)
        return remote(ref, ref, (gs_sem, gr_sem), g, to_m)

    def forward_copy(g):
        ref = view(a_ref, g, mine, H)
        return remote(ref, ref, (fs_sem, fr_sem), g, to_m)

    def scatter(g):
        p0, count, col0, width = GROUPS[g]
        mate_copy(g).wait_recv()
        for p in range(p0, p0 + count):
            gp_ref[p, pl.ds(mine, H), col0:col0 + width] += mate_ref[p, :, col0:col0 + width]
        for rel in range(1, 8):
            part_copy(g, rel).start()

    def reduce(g):
        p0, count, col0, width = GROUPS[g]
        part_all(g).wait_recv()
        for p in range(p0, p0 + count):
            total = gp_ref[p, pl.ds(slice_at, 8), col0:col0 + width]
            for rel in range(1, 8):
                total += part_ref[p, 8 * (rel - 1):8 * rel, col0:col0 + width]
            a_ref[p, pl.ds(slice_at, 8), col0:col0 + width] = total
        for rel in range(1, 8):
            row_copy(g, rel).start()

    def forward(g):
        row_all(g).wait_recv()
        forward_copy(g).start()

    for g, (p0, count, col0, width) in enumerate(GROUPS):
        for p in range(p0, p0 + count):
            gp_ref[p, :, col0:col0 + width] = lax.dot_general(
                wt_ref[B * p:B * (p + 1), :], wt_ref[col0:col0 + width, :], (((1,), (1,)), ((), ())), preferred_element_type=f32)
        mate_copy(g).start()
        if g == 1:
            scatter(0)
    done = lambda g: forward_copy(g).wait_recv()
    scatter(1)
    reduce(0)
    for i in range(NB):
        g_ref[B * i:B * (i + 1), N:] = ft_ref[B * i:B * (i + 1), :].astype(f32)
    var_ref[...] = jnp.zeros_like(var_ref)
    ul_ref[...] = jnp.zeros_like(ul_ref)
    ur_ref[...] = jnp.zeros_like(ur_ref)
    scatter(2)
    scatter(3)
    forward(0)
    reduce(1)
    done(0)
    at_start = {3: [(forward, 5)]}
    before_rows = {1: [(forward, 1), (done, 1), (forward, 2), (scatter, 5)], 2: [(done, 3), (reduce, 5)]}
    before_block = {0: [(reduce, 2)], 1: [(done, 2), (reduce, 4)], 2: [(forward, 4), (done, 4), (scatter, 7)], 3: [(done, 5), (reduce, 7)], 4: [(done, 6), (forward, 7)], 6: [(done, 7)]}
    middle = {
        4: {0: [(scatter, 4)]},
        8: {0: [(reduce, 3)], 1: [(forward, 3)], 2: [(reduce, 6)]},
        12: {1: [(scatter, 6)], 3: [(forward, 6)]},
    }

    def run(table, k):
        for key, steps in table.items():
            @pl.when(k == key)
            def _(steps=steps):
                for step, g in steps:
                    step(g)

    diag_r = lax.broadcasted_iota(jnp.int32, (8, B), 0)
    diag_c = lax.broadcasted_iota(jnp.int32, (8, B), 1)
    CW = 512

    def row_panel(p, c0, with_a, lcat):
        g = g_ref[pl.ds(pl.multiple_of(p * B, B), B), c0:c0 + CW]
        if with_a:
            g = g + a_ref[p, :, c0:c0 + CW] * f32(1.0 / ROWS)
        gh, gl = split3(g)
        u = jnp.dot(lcat, jnp.concatenate([gh, gh, gl], axis=0), preferred_element_type=f32)
        uh, ul = split3(u)
        ur_ref[0:B, c0:c0 + CW] = uh
        ur_ref[B:2 * B, c0:c0 + CW] = uh
        ur_ref[2 * B:, c0:c0 + CW] = ul
        if with_a:
            for t in range(CW // B):
                th, tl = split3(u[:, B * t:B * (t + 1)].T)
                r0 = c0 + B * t
                ul_ref[r0:r0 + B, 0:B] = th
                ul_ref[r0:r0 + B, B:2 * B] = tl
                ul_ref[r0:r0 + B, 2 * B:] = th
        else:
            var_ref[...] += jnp.sum(u * u, axis=0, keepdims=True)

    def inverse_factor():
        lh, ll = split3(linv_ref[...])
        return jnp.concatenate([lh, ll, lh], axis=1)

    @pl.loop(0, NB)
    def _(k):
        k0 = pl.multiple_of(k * B, B)
        run(at_start, k)

        @pl.when(k > 0)
        def _():
            lcat = inverse_factor()
            row_panel(k - 1, N, False, lcat)
            run(before_rows, k)
            row_panel(k - 1, CW, True, lcat)

            @pl.when(k < NB // 2)
            def _():
                row_panel(k - 1, 0, True, lcat)
            lhs = ul_ref[pl.ds(k0, B), :]
            for c0 in (CW, N):
                g_ref[pl.ds(k0, B), c0:c0 + CW] -= jnp.dot(lhs, ur_ref[:, c0:c0 + CW], preferred_element_type=f32)

            @pl.when(k < NB // 2)
            def _():
                g_ref[pl.ds(k0, B), 0:CW] -= jnp.dot(lhs, ur_ref[:, 0:CW], preferred_element_type=f32)
        run(before_block, k)
        pr = prior_ref[:, pl.ds(k0, B)]
        S = []
        for i in range(16):
            s = g_ref[pl.ds(k0 + 8 * i, 8), pl.ds(k0, B)] + a_ref[k, pl.ds(8 * i, 8), pl.ds(k0, B)] * f32(1.0 / ROWS)
            S.append(s + jnp.where(diag_c == diag_r + 8 * i, pr, f32(0)))
        rows = pl.ds(pl.multiple_of(k0 + B, B), SLAB)

        def hook(b):
            if b in middle:
                run(middle[b], k)
            if b % 2 == 1 and b // 2 < W // 256:
                cols = slice(b // 2 * 256, (b // 2 + 1) * 256)
                g_ref[rows, cols] -= jnp.dot(ul_ref[rows, :], ur_ref[:, cols], preferred_element_type=f32)
        out = diag_inverse(S, hook)
        for i in range(16):
            linv_ref[pl.ds(8 * i, 8), :] = out[i]

    row_panel(NB - 1, N, False, inverse_factor())
    var = var_ref[...] * (4.0 / P_SIZE)
    moder = jnp.exp(logits / jnp.sqrt(1.0 + var))
    moder = moder / jnp.sum(moder, axis=0, keepdims=True)
    mod_ref[0:C, :] = moder

    def member_copy(rel):
        return pltpu.make_async_remote_copy(
            src_ref=mod_ref, dst_ref=got_ref.at[rel - 1], send_sem=es_sem, recv_sem=er_sem,
            device_id=(members[rel - 1], d), device_id_type=MESH)

    for rel in range(1, MEMBERS):
        member_copy(rel).start()
    for g in range(len(GROUPS)):
        mate_copy(g).wait_send()
        part_all(g).wait_send()
        row_all(g).wait_send()
        forward_copy(g).wait_send()
    every = pltpu.make_async_remote_copy(
        src_ref=got_ref, dst_ref=got_ref, send_sem=es_sem, recv_sem=er_sem, device_id=(m, to_m), device_id_type=MESH)
    every.wait_recv()
    total = moder
    for rel in range(1, MEMBERS):
        total += got_ref[rel - 1, 0:C, :]
    out_ref[0:C, :] = total * f32(1.0 / MEMBERS)
    out_ref[C:C + 1, :] = var
    every.wait_send()
    for cp in sends:
        cp.wait_send()


def laplace(hidden, proj, hw, hb, prior, labels, cw):
    vm = pl.BlockSpec(memory_space=pltpu.VMEM)
    any_ = pl.BlockSpec(memory_space=pl.ANY)
    dma = pltpu.SemaphoreType.DMA
    return pl.pallas_call(
        laplace_kernel,
        out_shape=jax.ShapeDtypeStruct((16, R_), f32),
        in_specs=[any_, any_, vm, vm, vm, vm, vm],
        out_specs=vm,
        scratch_shapes=[
            pltpu.VMEM((R_, 4096), bf16),
            pltpu.VMEM((8, 2 * KB, P_SIZE), bf16),
            pltpu.VMEM((R_, P_SIZE), f32),
            pltpu.VMEM((N, R_), bf16),
            pltpu.VMEM((N, R_), bf16),
            pltpu.VMEM((NB, B, N), f32),
            pltpu.VMEM((NB, B // 2, N), f32),
            pltpu.VMEM((NB, 56, N), f32),
            pltpu.VMEM((NB, B, N), f32),
            pltpu.VMEM((1, R_), f32),
            pltpu.VMEM((N + SLAB, W), f32),
            pltpu.VMEM((B, B), f32),
            pltpu.VMEM((N + SLAB, 3 * B), bf16),
            pltpu.VMEM((3 * B, W), bf16),
            pltpu.VMEM((16, R_), f32),
            pltpu.VMEM((MEMBERS - 1, 16, R_), f32),
            dma((2,)), dma((30,)), dma((16, 2)),
            dma((8,)), dma((8,)), dma((8,)), dma((8,)), dma((8,)), dma((8,)), dma((8,)), dma((8,)),
            dma, dma,
        ],
        compiler_params=pltpu.CompilerParams(
            collective_id=0, has_side_effects=True, vmem_limit_bytes=56 * 1024 * 1024),
    )(hidden, proj, hw, hb, prior, labels, cw)


def finish_kernel(pack_ref, var_ref, ens_ref):
    ens_ref[...] = pack_ref[0:C, :]
    var_ref[...] = pack_ref[C:C + 1, :]


def body(hidden, projection, head_weight, head_bias, prior_precision, labels, category_weight):
    pack = laplace(
        hidden[0], projection[0], head_weight[0], head_bias, prior_precision, labels[None, :], category_weight[None, :])
    vm = pl.BlockSpec(memory_space=pltpu.VMEM)
    return pl.pallas_call(
        finish_kernel,
        out_shape=(jax.ShapeDtypeStruct((1, R_), f32), jax.ShapeDtypeStruct((C, R_), f32)),
        in_specs=[vm],
        out_specs=(vm, vm),
    )(pack)


def solution(mesh):
    return jax.shard_map(
        body,
        mesh=mesh,
        in_specs=(
            P("member", "dp", None),
            P("member", "dp", None),
            P("member", None, None),
            P("member", None),
            P("member", None),
            P("dp"),
            P(),
        ),
        out_specs=(P("member", "dp"), P(None, "dp")),
        check_vma=False,
    )
```

```python
import jax, jax.numpy as jnp
from jax import lax
from jax.experimental import pallas as pl
from jax.experimental.pallas import tpu as pltpu
from jax.sharding import PartitionSpec as P

N = 1024
P_SIZE = 1024
ROWS = 8192
B = 128
NB = N // B
R_ = 512
W = N + R_
f32 = jnp.float32
bf16 = jnp.bfloat16


def split3(x):
    hi = x.astype(bf16)
    lo = (x - hi.astype(f32)).astype(bf16)
    return hi, lo


SB = 4
NEXT = 1


def diag_inverse(S, hook=lambda b: None):
    G = 8
    n = B // G
    T = list(S)
    lane = lax.broadcasted_iota(jnp.int32, (G, B), 1)
    sub = lax.broadcasted_iota(jnp.int32, (G, B), 0)
    out = [None] * n
    held = []

    def column(t, j):
        return jnp.take_along_axis(t, jnp.full((G, B), j, jnp.int32), axis=1)

    def row(t, j):
        return jnp.broadcast_to(t[j:j + 1, :], (G, B))

    for b in range(n):
        hook(b)
        first = b - b % SB
        edge = min(first + SB + NEXT, n)
        cb = ahead if b else [column(T[b], G * b + k) for k in range(G)]
        below = range(b + 1, edge)
        cn = {i: [column(T[i], G * b + k) for k in range(G)] for i in below}
        if b < n - 1:
            ahead = [column(T[b + 1], G * (b + 1) + k) for k in range(G)]
        own = (lane >= G * b) & (lane < G * b + G)
        tn = {i: jnp.where(own, f32(0), T[i]) for i in below}
        rb = T[b]
        qb = jnp.where(lane < G * b, rb, jnp.where(lane == sub + G * b, f32(1), f32(0)))
        dv = jnp.ones((G, B), f32)
        iv = jnp.ones((G, B), f32)
        for j in range(G):
            p = row(cb[j], j)
            inv = 1.0 / p
            dv = jnp.where(sub == j, p, dv)
            iv = jnp.where(sub == j, inv, iv)
            m = jnp.where(sub > j, cb[j] * inv, f32(0))
            mn = {i: cn[i][j] * inv for i in below}
            if b < n - 1:
                for k in range(G):
                    ahead[k] = ahead[k] - mn[b + 1] * row(cn[b + 1][j], k)
            for k in range(j + 1, G):
                r = row(cb[k], j)
                cb[k] = cb[k] - m * r
                for i in below:
                    cn[i][k] = cn[i][k] - mn[i] * r
            q = row(qb, j)
            if b < n - 1:
                r = row(rb, j)
                full = jnp.where(lane < G * b + G, q, r)
                for i in below:
                    tn[i] = tn[i] - mn[i] * full
                if j < G - 1:
                    rb = rb - m * r
            if j < G - 1:
                qb = qb - m * q
        out[b] = qb * lax.rsqrt(dv)
        for i in below:
            T[i] = tn[i]
        if edge < n:
            end = G * (first + SB)
            held.append((rb * iv, jnp.where(lane < G * b + G, qb, jnp.where(lane < end, f32(0), rb))))
            if b == first + SB - 1:
                left = jnp.concatenate([x for x, _ in held], axis=0)
                right = jnp.concatenate([y for _, y in held], axis=0)
                lh, ll = split3(left)
                rh, rl = split3(right)
                prod = lax.dot_general(
                    jnp.concatenate([lh, lh, ll], axis=0), jnp.concatenate([rh, rl, rh], axis=0),
                    (((0,), (0,)), ((), ())), preferred_element_type=f32)
                region = (lane >= G * first) & (lane < end)
                for i in range(edge, n):
                    T[i] = jnp.where(region, f32(0), T[i]) - prod[G * i:G * i + G, :]
                held = []
    return out


MESH = pl.DeviceIdType.MESH
C = 14
MEMBERS = 8
GROUPS = (
    (0, 1, 0, 128),
    (0, 1, 128, 896),
    (1, 1, 128, 128),
    (1, 1, 256, 768),
    (2, 1, 256, 768),
    (3, 1, 384, 640),
    (4, 2, 512, 512),
    (6, 2, 768, 256),
)
KB = 256
SLAB = 6 * B
MN = 512


def laplace_kernel(hid_ref, proj_ref, hw_ref, hb_ref, prior_ref, lab_ref, cw_ref, out_ref,
                   h_ref, buf_ref, acc_ref, ft_ref, wt_ref, gp_ref, mate_ref, part_ref, a_ref, var_ref,
                   g_ref, linv_ref, ul_ref, ur_ref, mod_ref, got_ref,
                   loc_sem, send_sem, recv_sem, ms_sem, mr_sem, ss_sem, sr_sem, gs_sem, gr_sem, fs_sem, fr_sem,
                   es_sem, er_sem):
    m = lax.axis_index("member")
    d = lax.axis_index("dp")
    c = lax.rem(d, 2)
    x = lax.rem(d // 2, 4)
    yh = d // 8

    def dp(dy, dx, t):
        yy = yh if dy == 0 else 1 - yh
        cc = c if t == 0 else 1 - c
        return (yy * 4 + lax.rem(x + dx, 4)) * 2 + cc

    to_r, to_l, to_y, to_m = dp(0, 1, 0), dp(0, 3, 0), dp(1, 0, 0), dp(0, 0, 1)
    me = d
    own_copy = pltpu.make_async_copy(proj_ref, buf_ref.at[d // 2, pl.ds(pl.multiple_of(c * KB, KB), KB), :], loc_sem.at[0])
    own_copy.start()
    hid_copy = pltpu.make_async_copy(hid_ref, h_ref, loc_sem.at[1])
    hid_copy.start()
    bar = pltpu.get_barrier_semaphore()
    chip = d // 2
    peers = [lax.rem(chip + rel, 8) * 2 + c for rel in range(1, 8)]
    for t in peers + [to_m]:
        pl.semaphore_signal(bar, inc=1, device_id=(m, t), device_id_type=MESH)
    members = [lax.rem(m + rel, MEMBERS) for rel in range(1, MEMBERS)]
    for t in members:
        pl.semaphore_signal(bar, inc=1, device_id=(t, d), device_id_type=MESH)
    pl.semaphore_wait(bar, 15)
    own_copy.wait()
    sends = []

    def half(s, h):
        return buf_ref.at[s // 2, pl.ds(pl.multiple_of(lax.rem(s, 2) * KB + h * (KB // 2), KB // 2), KB // 2), :]

    def copy(s, h, to, i):
        return pltpu.make_async_remote_copy(
            src_ref=half(s, h), dst_ref=half(s, h), send_sem=send_sem.at[i], recv_sem=recv_sem.at[s, h],
            device_id=(m, to), device_id_type=MESH)

    def send(to, s, h):
        cp = copy(s, h, to, len(sends))
        cp.start()
        sends.append(cp)

    def wait(s, h):
        copy(s, h, to_m, 0).wait_recv()

    def mm(s, first=False):
        place = s // 2
        k0 = pl.multiple_of(place * 2 * KB, 2 * KB)

        @pl.loop(0, P_SIZE // MN)
        def _(n):
            n0 = pl.multiple_of(n * MN, MN)
            r = jnp.dot(h_ref[:, pl.ds(k0, 2 * KB)], buf_ref[place, :, pl.ds(n0, MN)], preferred_element_type=f32)
            if first:
                acc_ref[:, pl.ds(n0, MN)] = r
            else:
                acc_ref[:, pl.ds(n0, MN)] += r

    def mm_half(s):
        k0 = pl.multiple_of(s * KB, KB)
        row0 = pl.multiple_of(lax.rem(s, 2) * KB, KB)

        @pl.loop(0, P_SIZE // MN)
        def _(n):
            n0 = pl.multiple_of(n * MN, MN)
            acc_ref[:, pl.ds(n0, MN)] += jnp.dot(
                h_ref[:, pl.ds(k0, KB)], buf_ref[s // 2, pl.ds(row0, KB), pl.ds(n0, MN)], preferred_element_type=f32)

    left, right, anti, part = dp(0, 3, 0), dp(0, 1, 0), dp(0, 2, 0), dp(1, 0, 0)
    far_l, far_r, far_a = dp(1, 3, 0), dp(1, 1, 0), dp(1, 2, 0)

    def mate_mm(dy, dx, first=False):
        s = dp(dy, dx, 1)
        wait(s, 0)
        wait(s, 1)
        mm(s, first)

    send(to_r, me, 0)
    send(to_l, me, 1)
    send(to_y, me, 0)
    send(to_y, me, 1)
    send(to_r, me, 1)
    send(to_l, me, 0)
    send(to_m, me, 0)
    send(to_m, me, 1)
    for i in range(NB):
        g_ref[B * i:B * (i + 1), :N] = jnp.zeros((B, N), f32)
    ul_ref[...] = jnp.zeros_like(ul_ref)
    ur_ref[...] = jnp.zeros_like(ur_ref)
    hid_copy.wait()
    wait(left, 0)
    send(to_r, left, 0)
    send(to_y, left, 0)
    wait(right, 1)
    send(to_l, right, 1)
    send(to_y, right, 1)
    send(to_m, left, 0)
    send(to_m, right, 1)
    wait(part, 0)
    send(to_l, part, 0)
    wait(part, 1)
    send(to_r, part, 1)
    send(to_m, part, 0)
    send(to_m, part, 1)
    wait(left, 1)
    send(to_m, left, 1)
    wait(right, 0)
    send(to_m, right, 0)
    mate_mm(0, 0, True)
    mate_mm(0, 3)
    mate_mm(0, 1)
    wait(anti, 0)
    send(to_m, anti, 0)
    wait(anti, 1)
    send(to_m, anti, 1)
    wait(far_l, 0)
    send(to_r, far_l, 0)
    wait(far_r, 1)
    send(to_l, far_r, 1)
    send(to_m, far_l, 0)
    send(to_m, far_r, 1)
    mate_mm(1, 0)
    mate_mm(0, 2)
    wait(far_l, 1)
    send(to_m, far_l, 1)
    wait(far_r, 0)
    send(to_m, far_r, 0)
    mate_mm(1, 3)
    mate_mm(1, 1)
    wait(far_a, 0)
    send(to_m, far_a, 0)
    wait(far_a, 1)
    send(to_m, far_a, 1)
    mm_half(far_a)
    last = dp(1, 2, 1)
    wait(last, 0)
    wait(last, 1)
    mm_half(last)

    for j in range(NB):
        ft_ref[B * j:B * (j + 1), :] = acc_ref[:, B * j:B * (j + 1)].T.astype(bf16)
    eye = lax.broadcasted_iota(jnp.int32, (C, C), 0) == lax.broadcasted_iota(jnp.int32, (C, C), 1)
    bias = jnp.sum(jnp.where(eye, hb_ref[...], f32(0)), axis=1, keepdims=True)
    weight = jnp.sum(jnp.where(eye, cw_ref[...].astype(f32), f32(0)), axis=1, keepdims=True)
    logits = jnp.dot(hw_ref[...], ft_ref[...], preferred_element_type=f32) + bias
    cat = lax.broadcasted_iota(jnp.int32, (C, R_), 0)
    row_weight = jnp.sum(jnp.where(cat == lab_ref[...], weight, f32(0)), axis=0, keepdims=True)
    expo = jnp.exp(logits)
    probs = expo / jnp.sum(expo, axis=0, keepdims=True)
    curv = row_weight * (1.0 - jnp.sum(probs * probs, axis=0, keepdims=True))
    root = jnp.sqrt(curv)
    for j in range(NB):
        wt_ref[B * j:B * (j + 1), :] = (ft_ref[B * j:B * (j + 1), :].astype(f32) * root).astype(bf16)

    H = B // 2
    mine = pl.multiple_of(c * H, H)
    other = pl.multiple_of((1 - c) * H, H)
    slice_at = pl.multiple_of(mine + 8 * chip, 8)

    def remote(src, dst, sems, g, to):
        return pltpu.make_async_remote_copy(
            src_ref=src, dst_ref=dst, send_sem=sems[0].at[g], recv_sem=sems[1].at[g], device_id=(m, to), device_id_type=MESH)

    def view(ref, g, row0, rows):
        p0, count, col0, width = GROUPS[g]
        return ref.at[pl.ds(p0, count), pl.ds(row0, rows), pl.ds(col0, width)]

    def mate_copy(g):
        return remote(view(gp_ref, g, other, H), view(mate_ref, g, 0, H), (ms_sem, mr_sem), g, to_m)

    def part_copy(g, rel):
        to = lax.rem(chip + rel, 8)
        return remote(view(gp_ref, g, pl.multiple_of(mine + 8 * to, 8), 8), view(part_ref, g, 8 * (rel - 1), 8),
                      (ss_sem, sr_sem), g, to * 2 + c)

    def part_all(g):
        return remote(view(part_ref, g, 0, 56), view(part_ref, g, 0, 56), (ss_sem, sr_sem), g, to_m)

    def row_copy(g, rel):
        ref = view(a_ref, g, slice_at, 8)
        return remote(ref, ref, (gs_sem, gr_sem), g, lax.rem(chip + rel, 8) * 2 + c)

    def row_all(g):
        ref = view(a_ref, g, mine, 56)
        return remote(ref, ref, (gs_sem, gr_sem), g, to_m)

    def forward_copy(g):
        ref = view(a_ref, g, mine, H)
        return remote(ref, ref, (fs_sem, fr_sem), g, to_m)

    def scatter(g):
        p0, count, col0, width = GROUPS[g]
        mate_copy(g).wait_recv()
        for p in range(p0, p0 + count):
            gp_ref[p, pl.ds(mine, H), col0:col0 + width] += mate_ref[p, :, col0:col0 + width]
        for rel in range(1, 8):
            part_copy(g, rel).start()

    def reduce(g):
        p0, count, col0, width = GROUPS[g]
        part_all(g).wait_recv()
        for p in range(p0, p0 + count):
            total = gp_ref[p, pl.ds(slice_at, 8), col0:col0 + width]
            for rel in range(1, 8):
                total += part_ref[p, 8 * (rel - 1):8 * rel, col0:col0 + width]
            a_ref[p, pl.ds(slice_at, 8), col0:col0 + width] = total
        for rel in range(1, 8):
            row_copy(g, rel).start()

    def forward(g):
        row_all(g).wait_recv()
        forward_copy(g).start()

    for g, (p0, count, col0, width) in enumerate(GROUPS):
        for p in range(p0, p0 + count):
            gp_ref[p, :, col0:col0 + width] = lax.dot_general(
                wt_ref[B * p:B * (p + 1), :], wt_ref[col0:col0 + width, :], (((1,), (1,)), ((), ())), preferred_element_type=f32)
        mate_copy(g).start()
        if g == 1:
            scatter(0)
        if g == 4:
            scatter(1)
        if g == 5:
            reduce(0)
    done = lambda g: forward_copy(g).wait_recv()
    for i in range(NB):
        g_ref[B * i:B * (i + 1), N:] = ft_ref[B * i:B * (i + 1), :].astype(f32)
    var_ref[...] = jnp.zeros_like(var_ref)
    scatter(2)
    scatter(3)
    forward(0)
    reduce(1)
    done(0)
    at_start = {3: [(forward, 5)]}
    before_rows = {1: [(forward, 1), (done, 1), (forward, 2), (scatter, 5)], 2: [(done, 3), (reduce, 5)]}
    before_block = {0: [(reduce, 2)], 1: [(done, 2), (reduce, 4)], 2: [(forward, 4), (done, 4), (scatter, 7)], 3: [(done, 5), (reduce, 7)], 4: [(done, 6), (forward, 7)], 6: [(done, 7)]}
    middle = {
        4: {0: [(scatter, 4)]},
        8: {0: [(reduce, 3)], 1: [(forward, 3)], 2: [(reduce, 6)]},
        12: {1: [(scatter, 6)], 3: [(forward, 6)]},
    }

    def run(table, k):
        for key, steps in table.items():
            @pl.when(k == key)
            def _(steps=steps):
                for step, g in steps:
                    step(g)

    diag_r = lax.broadcasted_iota(jnp.int32, (8, B), 0)
    diag_c = lax.broadcasted_iota(jnp.int32, (8, B), 1)
    CW = 512

    def row_panel(p, c0, with_a, lcat):
        g = g_ref[pl.ds(pl.multiple_of(p * B, B), B), c0:c0 + CW]
        if with_a:
            g = g + a_ref[p, :, c0:c0 + CW] * f32(1.0 / ROWS)
        gh, gl = split3(g)
        u = jnp.dot(lcat, jnp.concatenate([gh, gh, gl], axis=0), preferred_element_type=f32)
        uh, ul = split3(u)
        ur_ref[0:B, c0:c0 + CW] = uh
        ur_ref[B:2 * B, c0:c0 + CW] = uh
        ur_ref[2 * B:, c0:c0 + CW] = ul
        if with_a:
            for t in range(CW // B):
                th, tl = split3(u[:, B * t:B * (t + 1)].T)
                r0 = c0 + B * t
                ul_ref[r0:r0 + B, 0:B] = th
                ul_ref[r0:r0 + B, B:2 * B] = tl
                ul_ref[r0:r0 + B, 2 * B:] = th
        else:
            var_ref[...] += jnp.sum(u * u, axis=0, keepdims=True)

    def inverse_factor():
        lh, ll = split3(linv_ref[...])
        return jnp.concatenate([lh, ll, lh], axis=1)

    @pl.loop(0, NB)
    def _(k):
        k0 = pl.multiple_of(k * B, B)
        run(at_start, k)

        @pl.when(k > 0)
        def _():
            lcat = inverse_factor()
            row_panel(k - 1, N, False, lcat)
            run(before_rows, k)
            row_panel(k - 1, CW, True, lcat)

            @pl.when(k < NB // 2)
            def _():
                row_panel(k - 1, 0, True, lcat)
            lhs = ul_ref[pl.ds(k0, B), :]
            for c0 in (CW, N):
                g_ref[pl.ds(k0, B), c0:c0 + CW] -= jnp.dot(lhs, ur_ref[:, c0:c0 + CW], preferred_element_type=f32)

            @pl.when(k < NB // 2)
            def _():
                g_ref[pl.ds(k0, B), 0:CW] -= jnp.dot(lhs, ur_ref[:, 0:CW], preferred_element_type=f32)
        run(before_block, k)
        pr = prior_ref[:, pl.ds(k0, B)]
        S = []
        for i in range(16):
            s = g_ref[pl.ds(k0 + 8 * i, 8), pl.ds(k0, B)] + a_ref[k, pl.ds(8 * i, 8), pl.ds(k0, B)] * f32(1.0 / ROWS)
            S.append(s + jnp.where(diag_c == diag_r + 8 * i, pr, f32(0)))
        rows = pl.ds(pl.multiple_of(k0 + B, B), SLAB)

        def hook(b):
            if b in middle:
                run(middle[b], k)
            if b % 2 == 1 and b // 2 < W // 256:
                cols = slice(b // 2 * 256, (b // 2 + 1) * 256)
                g_ref[rows, cols] -= jnp.dot(ul_ref[rows, :], ur_ref[:, cols], preferred_element_type=f32)
        out = diag_inverse(S, hook)
        for i in range(16):
            linv_ref[pl.ds(8 * i, 8), :] = out[i]

    row_panel(NB - 1, N, False, inverse_factor())
    var = var_ref[...] * (4.0 / P_SIZE)
    moder = jnp.exp(logits / jnp.sqrt(1.0 + var))
    moder = moder / jnp.sum(moder, axis=0, keepdims=True)
    mod_ref[0:C, :] = moder

    def member_copy(rel):
        return pltpu.make_async_remote_copy(
            src_ref=mod_ref, dst_ref=got_ref.at[rel - 1], send_sem=es_sem, recv_sem=er_sem,
            device_id=(members[rel - 1], d), device_id_type=MESH)

    for rel in range(1, MEMBERS):
        member_copy(rel).start()
    for g in range(len(GROUPS)):
        mate_copy(g).wait_send()
        part_all(g).wait_send()
        row_all(g).wait_send()
        forward_copy(g).wait_send()
    every = pltpu.make_async_remote_copy(
        src_ref=got_ref, dst_ref=got_ref, send_sem=es_sem, recv_sem=er_sem, device_id=(m, to_m), device_id_type=MESH)
    every.wait_recv()
    total = moder
    for rel in range(1, MEMBERS):
        total += got_ref[rel - 1, 0:C, :]
    out_ref[0:C, :] = total * f32(1.0 / MEMBERS)
    out_ref[C:C + 1, :] = var
    every.wait_send()
    for cp in sends:
        cp.wait_send()


def laplace(hidden, proj, hw, hb, prior, labels, cw):
    vm = pl.BlockSpec(memory_space=pltpu.VMEM)
    any_ = pl.BlockSpec(memory_space=pl.ANY)
    dma = pltpu.SemaphoreType.DMA
    return pl.pallas_call(
        laplace_kernel,
        out_shape=jax.ShapeDtypeStruct((16, R_), f32),
        in_specs=[any_, any_, vm, vm, vm, vm, vm],
        out_specs=vm,
        scratch_shapes=[
            pltpu.VMEM((R_, 4096), bf16),
            pltpu.VMEM((8, 2 * KB, P_SIZE), bf16),
            pltpu.VMEM((R_, P_SIZE), f32),
            pltpu.VMEM((N, R_), bf16),
            pltpu.VMEM((N, R_), bf16),
            pltpu.VMEM((NB, B, N), f32),
            pltpu.VMEM((NB, B // 2, N), f32),
            pltpu.VMEM((NB, 56, N), f32),
            pltpu.VMEM((NB, B, N), f32),
            pltpu.VMEM((1, R_), f32),
            pltpu.VMEM((N + SLAB, W), f32),
            pltpu.VMEM((B, B), f32),
            pltpu.VMEM((N + SLAB, 3 * B), bf16),
            pltpu.VMEM((3 * B, W), bf16),
            pltpu.VMEM((16, R_), f32),
            pltpu.VMEM((MEMBERS - 1, 16, R_), f32),
            dma((2,)), dma((30,)), dma((16, 2)),
            dma((8,)), dma((8,)), dma((8,)), dma((8,)), dma((8,)), dma((8,)), dma((8,)), dma((8,)),
            dma, dma,
        ],
        compiler_params=pltpu.CompilerParams(
            collective_id=0, has_side_effects=True, vmem_limit_bytes=56 * 1024 * 1024),
    )(hidden, proj, hw, hb, prior, labels, cw)


def finish_kernel(pack_ref, var_ref, ens_ref):
    ens_ref[...] = pack_ref[0:C, :]
    var_ref[...] = pack_ref[C:C + 1, :]


def body(hidden, projection, head_weight, head_bias, prior_precision, labels, category_weight):
    pack = laplace(
        hidden[0], projection[0], head_weight[0], head_bias, prior_precision, labels[None, :], category_weight[None, :])
    vm = pl.BlockSpec(memory_space=pltpu.VMEM)
    return pl.pallas_call(
        finish_kernel,
        out_shape=(jax.ShapeDtypeStruct((1, R_), f32), jax.ShapeDtypeStruct((C, R_), f32)),
        in_specs=[vm],
        out_specs=(vm, vm),
    )(pack)


def solution(mesh):
    return jax.shard_map(
        body,
        mesh=mesh,
        in_specs=(
            P("member", "dp", None),
            P("member", "dp", None),
            P("member", None, None),
            P("member", None),
            P("member", None),
            P("dp"),
            P(),
        ),
        out_specs=(P("member", "dp"), P(None, "dp")),
        check_vma=False,
    )
```

```python
import jax, jax.numpy as jnp
from jax import lax
from jax.experimental import pallas as pl
from jax.experimental.pallas import tpu as pltpu
from jax.sharding import PartitionSpec as P

N = 1024
P_SIZE = 1024
ROWS = 8192
B = 128
NB = N // B
R_ = 512
W = N + R_
f32 = jnp.float32
bf16 = jnp.bfloat16


def split3(x):
    hi = x.astype(bf16)
    lo = (x - hi.astype(f32)).astype(bf16)
    return hi, lo


SB = 4
NEXT = 1


def diag_inverse(S, hook=lambda b: None):
    G = 8
    n = B // G
    T = list(S)
    lane = lax.broadcasted_iota(jnp.int32, (G, B), 1)
    sub = lax.broadcasted_iota(jnp.int32, (G, B), 0)
    out = [None] * n
    held = []

    def column(t, j):
        return jnp.take_along_axis(t, jnp.full((G, B), j, jnp.int32), axis=1)

    def row(t, j):
        return jnp.broadcast_to(t[j:j + 1, :], (G, B))

    for b in range(n):
        hook(b)
        first = b - b % SB
        edge = min(first + SB + NEXT, n)
        cb = ahead if b else [column(T[b], G * b + k) for k in range(G)]
        below = range(b + 1, edge)
        cn = {i: [column(T[i], G * b + k) for k in range(G)] for i in below}
        if b < n - 1:
            ahead = [column(T[b + 1], G * (b + 1) + k) for k in range(G)]
        own = (lane >= G * b) & (lane < G * b + G)
        tn = {i: jnp.where(own, f32(0), T[i]) for i in below}
        rb = T[b]
        qb = jnp.where(lane < G * b, rb, jnp.where(lane == sub + G * b, f32(1), f32(0)))
        dv = jnp.ones((G, B), f32)
        iv = jnp.ones((G, B), f32)
        for j in range(G):
            p = row(cb[j], j)
            inv = 1.0 / p
            dv = jnp.where(sub == j, p, dv)
            iv = jnp.where(sub == j, inv, iv)
            m = jnp.where(sub > j, cb[j] * inv, f32(0))
            mn = {i: cn[i][j] * inv for i in below}
            if b < n - 1:
                for k in range(G):
                    ahead[k] = ahead[k] - mn[b + 1] * row(cn[b + 1][j], k)
            for k in range(j + 1, G):
                r = row(cb[k], j)
                cb[k] = cb[k] - m * r
                for i in below:
                    cn[i][k] = cn[i][k] - mn[i] * r
            q = row(qb, j)
            if b < n - 1:
                r = row(rb, j)
                full = jnp.where(lane < G * b + G, q, r)
                for i in below:
                    tn[i] = tn[i] - mn[i] * full
                if j < G - 1:
                    rb = rb - m * r
            if j < G - 1:
                qb = qb - m * q
        out[b] = qb * lax.rsqrt(dv)
        for i in below:
            T[i] = tn[i]
        if edge < n:
            end = G * (first + SB)
            held.append((rb * iv, jnp.where(lane < G * b + G, qb, jnp.where(lane < end, f32(0), rb))))
            if b == first + SB - 1:
                left = jnp.concatenate([x for x, _ in held], axis=0)
                right = jnp.concatenate([y for _, y in held], axis=0)
                lh, ll = split3(left)
                rh, rl = split3(right)
                prod = lax.dot_general(
                    jnp.concatenate([lh, lh, ll], axis=0), jnp.concatenate([rh, rl, rh], axis=0),
                    (((0,), (0,)), ((), ())), preferred_element_type=f32)
                region = (lane >= G * first) & (lane < end)
                for i in range(edge, n):
                    T[i] = jnp.where(region, f32(0), T[i]) - prod[G * i:G * i + G, :]
                held = []
    return out


MESH = pl.DeviceIdType.MESH
C = 14
MEMBERS = 8
GROUPS = (
    (0, 1, 0, 128),
    (0, 1, 128, 896),
    (1, 1, 128, 128),
    (1, 1, 256, 768),
    (2, 1, 256, 768),
    (3, 1, 384, 640),
    (4, 2, 512, 512),
    (6, 2, 768, 256),
)
KB = 256
SLAB = 6 * B
MN = 512


def laplace_kernel(hid_ref, proj_ref, hw_ref, hb_ref, prior_ref, lab_ref, cw_ref, out_ref,
                   h_ref, buf_ref, acc_ref, ft_ref, wt_ref, gp_ref, mate_ref, part_ref, a_ref, var_ref,
                   g_ref, linv_ref, ul_ref, ur_ref, mod_ref, got_ref,
                   loc_sem, send_sem, recv_sem, ms_sem, mr_sem, ss_sem, sr_sem, gs_sem, gr_sem, fs_sem, fr_sem,
                   es_sem, er_sem):
    m = lax.axis_index("member")
    d = lax.axis_index("dp")
    c = lax.rem(d, 2)
    x = lax.rem(d // 2, 4)
    yh = d // 8

    def dp(dy, dx, t):
        yy = yh if dy == 0 else 1 - yh
        cc = c if t == 0 else 1 - c
        return (yy * 4 + lax.rem(x + dx, 4)) * 2 + cc

    to_r, to_l, to_y, to_m = dp(0, 1, 0), dp(0, 3, 0), dp(1, 0, 0), dp(0, 0, 1)
    me = d
    own_copy = pltpu.make_async_copy(proj_ref, buf_ref.at[d // 2, pl.ds(pl.multiple_of(c * KB, KB), KB), :], loc_sem.at[0])
    own_copy.start()
    hid_copy = pltpu.make_async_copy(hid_ref, h_ref, loc_sem.at[1])
    hid_copy.start()
    bar = pltpu.get_barrier_semaphore()
    chip = d // 2
    peers = [lax.rem(chip + rel, 8) * 2 + c for rel in range(1, 8)]
    members = [lax.rem(m + rel, MEMBERS) for rel in range(1, MEMBERS)]
    for t in members:
        pl.semaphore_signal(bar, inc=1, device_id=(t, d), device_id_type=MESH)
    for t in peers + [to_m]:
        pl.semaphore_signal(bar, inc=1, device_id=(m, t), device_id_type=MESH)
    pl.semaphore_wait(bar, 15)
    own_copy.wait()
    sends = []

    def half(s, h):
        return buf_ref.at[s // 2, pl.ds(pl.multiple_of(lax.rem(s, 2) * KB + h * (KB // 2), KB // 2), KB // 2), :]

    def copy(s, h, to, i):
        return pltpu.make_async_remote_copy(
            src_ref=half(s, h), dst_ref=half(s, h), send_sem=send_sem.at[i], recv_sem=recv_sem.at[s, h],
            device_id=(m, to), device_id_type=MESH)

    def send(to, s, h):
        cp = copy(s, h, to, len(sends))
        cp.start()
        sends.append(cp)

    def wait(s, h):
        copy(s, h, to_m, 0).wait_recv()

    def mm(s, first=False):
        place = s // 2
        k0 = pl.multiple_of(place * 2 * KB, 2 * KB)

        @pl.loop(0, P_SIZE // MN)
        def _(n):
            n0 = pl.multiple_of(n * MN, MN)
            r = jnp.dot(h_ref[:, pl.ds(k0, 2 * KB)], buf_ref[place, :, pl.ds(n0, MN)], preferred_element_type=f32)
            if first:
                acc_ref[:, pl.ds(n0, MN)] = r
            else:
                acc_ref[:, pl.ds(n0, MN)] += r

    def mm_half(s):
        k0 = pl.multiple_of(s * KB, KB)
        row0 = pl.multiple_of(lax.rem(s, 2) * KB, KB)

        @pl.loop(0, P_SIZE // MN)
        def _(n):
            n0 = pl.multiple_of(n * MN, MN)
            acc_ref[:, pl.ds(n0, MN)] += jnp.dot(
                h_ref[:, pl.ds(k0, KB)], buf_ref[s // 2, pl.ds(row0, KB), pl.ds(n0, MN)], preferred_element_type=f32)

    left, right, anti, part = dp(0, 3, 0), dp(0, 1, 0), dp(0, 2, 0), dp(1, 0, 0)
    far_l, far_r, far_a = dp(1, 3, 0), dp(1, 1, 0), dp(1, 2, 0)

    def mate_mm(dy, dx, first=False):
        s = dp(dy, dx, 1)
        wait(s, 0)
        wait(s, 1)
        mm(s, first)

    send(to_r, me, 0)
    send(to_l, me, 1)
    send(to_y, me, 0)
    send(to_y, me, 1)
    send(to_r, me, 1)
    send(to_l, me, 0)
    send(to_m, me, 0)
    send(to_m, me, 1)
    for i in range(NB):
        g_ref[B * i:B * (i + 1), :N] = jnp.zeros((B, N), f32)
    ul_ref[...] = jnp.zeros_like(ul_ref)
    ur_ref[...] = jnp.zeros_like(ur_ref)
    hid_copy.wait()
    wait(left, 0)
    send(to_r, left, 0)
    send(to_y, left, 0)
    wait(right, 1)
    send(to_l, right, 1)
    send(to_y, right, 1)
    send(to_m, left, 0)
    send(to_m, right, 1)
    wait(part, 0)
    send(to_l, part, 0)
    wait(part, 1)
    send(to_r, part, 1)
    send(to_m, part, 0)
    send(to_m, part, 1)
    wait(left, 1)
    send(to_m, left, 1)
    wait(right, 0)
    send(to_m, right, 0)
    mate_mm(0, 0, True)
    mate_mm(0, 3)
    mate_mm(0, 1)
    wait(anti, 0)
    send(to_m, anti, 0)
    wait(anti, 1)
    send(to_m, anti, 1)
    wait(far_l, 0)
    send(to_r, far_l, 0)
    wait(far_r, 1)
    send(to_l, far_r, 1)
    send(to_m, far_l, 0)
    send(to_m, far_r, 1)
    mate_mm(1, 0)
    mate_mm(0, 2)
    wait(far_l, 1)
    send(to_m, far_l, 1)
    wait(far_r, 0)
    send(to_m, far_r, 0)
    mate_mm(1, 3)
    mate_mm(1, 1)
    wait(far_a, 0)
    send(to_m, far_a, 0)
    wait(far_a, 1)
    send(to_m, far_a, 1)
    mm_half(far_a)
    last = dp(1, 2, 1)
    wait(last, 0)
    wait(last, 1)
    mm_half(last)

    for j in range(NB):
        ft_ref[B * j:B * (j + 1), :] = acc_ref[:, B * j:B * (j + 1)].T.astype(bf16)
    eye = lax.broadcasted_iota(jnp.int32, (C, C), 0) == lax.broadcasted_iota(jnp.int32, (C, C), 1)
    bias = jnp.sum(jnp.where(eye, hb_ref[...], f32(0)), axis=1, keepdims=True)
    weight = jnp.sum(jnp.where(eye, cw_ref[...].astype(f32), f32(0)), axis=1, keepdims=True)
    logits = jnp.dot(hw_ref[...], ft_ref[...], preferred_element_type=f32) + bias
    cat = lax.broadcasted_iota(jnp.int32, (C, R_), 0)
    row_weight = jnp.sum(jnp.where(cat == lab_ref[...], weight, f32(0)), axis=0, keepdims=True)
    expo = jnp.exp(logits)
    probs = expo / jnp.sum(expo, axis=0, keepdims=True)
    curv = row_weight * (1.0 - jnp.sum(probs * probs, axis=0, keepdims=True))
    root = jnp.sqrt(curv)
    for j in range(NB):
        wt_ref[B * j:B * (j + 1), :] = (ft_ref[B * j:B * (j + 1), :].astype(f32) * root).astype(bf16)

    H = B // 2
    mine = pl.multiple_of(c * H, H)
    other = pl.multiple_of((1 - c) * H, H)
    slice_at = pl.multiple_of(mine + 8 * chip, 8)

    def remote(src, dst, sems, g, to):
        return pltpu.make_async_remote_copy(
            src_ref=src, dst_ref=dst, send_sem=sems[0].at[g], recv_sem=sems[1].at[g], device_id=(m, to), device_id_type=MESH)

    def view(ref, g, row0, rows):
        p0, count, col0, width = GROUPS[g]
        return ref.at[pl.ds(p0, count), pl.ds(row0, rows), pl.ds(col0, width)]

    def mate_copy(g):
        return remote(view(gp_ref, g, other, H), view(mate_ref, g, 0, H), (ms_sem, mr_sem), g, to_m)

    def part_copy(g, rel):
        to = lax.rem(chip + rel, 8)
        return remote(view(gp_ref, g, pl.multiple_of(mine + 8 * to, 8), 8), view(part_ref, g, 8 * (rel - 1), 8),
                      (ss_sem, sr_sem), g, to * 2 + c)

    def part_all(g):
        return remote(view(part_ref, g, 0, 56), view(part_ref, g, 0, 56), (ss_sem, sr_sem), g, to_m)

    def row_copy(g, rel):
        ref = view(a_ref, g, slice_at, 8)
        return remote(ref, ref, (gs_sem, gr_sem), g, lax.rem(chip + rel, 8) * 2 + c)

    def row_all(g):
        ref = view(a_ref, g, mine, 56)
        return remote(ref, ref, (gs_sem, gr_sem), g, to_m)

    def forward_copy(g):
        ref = view(a_ref, g, mine, H)
        return remote(ref, ref, (fs_sem, fr_sem), g, to_m)

    def scatter(g):
        p0, count, col0, width = GROUPS[g]
        mate_copy(g).wait_recv()
        for p in range(p0, p0 + count):
            gp_ref[p, pl.ds(mine, H), col0:col0 + width] += mate_ref[p, :, col0:col0 + width]
        for rel in range(1, 8):
            part_copy(g, rel).start()

    def reduce(g):
        p0, count, col0, width = GROUPS[g]
        part_all(g).wait_recv()
        for p in range(p0, p0 + count):
            total = gp_ref[p, pl.ds(slice_at, 8), col0:col0 + width]
            for rel in range(1, 8):
                total += part_ref[p, 8 * (rel - 1):8 * rel, col0:col0 + width]
            a_ref[p, pl.ds(slice_at, 8), col0:col0 + width] = total
        for rel in range(1, 8):
            row_copy(g, rel).start()

    def forward(g):
        row_all(g).wait_recv()
        forward_copy(g).start()

    for g, (p0, count, col0, width) in enumerate(GROUPS):
        for p in range(p0, p0 + count):
            gp_ref[p, :, col0:col0 + width] = lax.dot_general(
                wt_ref[B * p:B * (p + 1), :], wt_ref[col0:col0 + width, :], (((1,), (1,)), ((), ())), preferred_element_type=f32)
        mate_copy(g).start()
        if g == 1:
            scatter(0)
        if g == 4:
            scatter(1)
        if g == 5:
            reduce(0)
    done = lambda g: forward_copy(g).wait_recv()
    for i in range(NB):
        g_ref[B * i:B * (i + 1), N:] = ft_ref[B * i:B * (i + 1), :].astype(f32)
    var_ref[...] = jnp.zeros_like(var_ref)
    scatter(2)
    scatter(3)
    forward(0)
    reduce(1)
    done(0)
    at_start = {3: [(forward, 5)]}
    before_rows = {1: [(forward, 1), (done, 1), (forward, 2), (scatter, 5)], 2: [(done, 3), (reduce, 5)]}
    before_block = {0: [(reduce, 2)], 1: [(done, 2), (reduce, 4)], 2: [(forward, 4), (done, 4), (scatter, 7)], 3: [(done, 5), (reduce, 7)], 4: [(done, 6), (forward, 7)], 6: [(done, 7)]}
    middle = {
        4: {0: [(scatter, 4)]},
        8: {0: [(reduce, 3)], 1: [(forward, 3)], 2: [(reduce, 6)]},
        12: {1: [(scatter, 6)], 3: [(forward, 6)]},
    }

    def run(table, k):
        for key, steps in table.items():
            @pl.when(k == key)
            def _(steps=steps):
                for step, g in steps:
                    step(g)

    diag_r = lax.broadcasted_iota(jnp.int32, (8, B), 0)
    diag_c = lax.broadcasted_iota(jnp.int32, (8, B), 1)
    CW = 512

    def row_panel(p, c0, with_a, lcat):
        g = g_ref[pl.ds(pl.multiple_of(p * B, B), B), c0:c0 + CW]
        if with_a:
            g = g + a_ref[p, :, c0:c0 + CW] * f32(1.0 / ROWS)
        gh, gl = split3(g)
        u = jnp.dot(lcat, jnp.concatenate([gh, gh, gl], axis=0), preferred_element_type=f32)
        uh, ul = split3(u)
        ur_ref[0:B, c0:c0 + CW] = uh
        ur_ref[B:2 * B, c0:c0 + CW] = uh
        ur_ref[2 * B:, c0:c0 + CW] = ul
        if with_a:
            for t in range(CW // B):
                th, tl = split3(u[:, B * t:B * (t + 1)].T)
                r0 = c0 + B * t
                ul_ref[r0:r0 + B, 0:B] = th
                ul_ref[r0:r0 + B, B:2 * B] = tl
                ul_ref[r0:r0 + B, 2 * B:] = th
        else:
            var_ref[...] += jnp.sum(u * u, axis=0, keepdims=True)

    def inverse_factor():
        lh, ll = split3(linv_ref[...])
        return jnp.concatenate([lh, ll, lh], axis=1)

    @pl.loop(0, NB)
    def _(k):
        k0 = pl.multiple_of(k * B, B)
        run(at_start, k)

        @pl.when(k > 0)
        def _():
            lcat = inverse_factor()
            row_panel(k - 1, N, False, lcat)
            run(before_rows, k)
            row_panel(k - 1, CW, True, lcat)

            @pl.when(k < NB // 2)
            def _():
                row_panel(k - 1, 0, True, lcat)
            lhs = ul_ref[pl.ds(k0, B), :]
            for c0 in (CW, N):
                g_ref[pl.ds(k0, B), c0:c0 + CW] -= jnp.dot(lhs, ur_ref[:, c0:c0 + CW], preferred_element_type=f32)

            @pl.when(k < NB // 2)
            def _():
                g_ref[pl.ds(k0, B), 0:CW] -= jnp.dot(lhs, ur_ref[:, 0:CW], preferred_element_type=f32)
        run(before_block, k)
        pr = prior_ref[:, pl.ds(k0, B)]
        S = []
        for i in range(16):
            s = g_ref[pl.ds(k0 + 8 * i, 8), pl.ds(k0, B)] + a_ref[k, pl.ds(8 * i, 8), pl.ds(k0, B)] * f32(1.0 / ROWS)
            S.append(s + jnp.where(diag_c == diag_r + 8 * i, pr, f32(0)))
        rows = pl.ds(pl.multiple_of(k0 + B, B), SLAB)

        def hook(b):
            if b in middle:
                run(middle[b], k)
            if b % 2 == 1 and b // 2 < W // 256:
                cols = slice(b // 2 * 256, (b // 2 + 1) * 256)
                g_ref[rows, cols] -= jnp.dot(ul_ref[rows, :], ur_ref[:, cols], preferred_element_type=f32)
        out = diag_inverse(S, hook)
        for i in range(16):
            linv_ref[pl.ds(8 * i, 8), :] = out[i]

    row_panel(NB - 1, N, False, inverse_factor())
    var = var_ref[...] * (4.0 / P_SIZE)
    moder = jnp.exp(logits / jnp.sqrt(1.0 + var))
    moder = moder / jnp.sum(moder, axis=0, keepdims=True)
    mod_ref[0:C, :] = moder

    def member_copy(rel):
        return pltpu.make_async_remote_copy(
            src_ref=mod_ref, dst_ref=got_ref.at[rel - 1], send_sem=es_sem, recv_sem=er_sem,
            device_id=(members[rel - 1], d), device_id_type=MESH)

    for rel in range(1, MEMBERS):
        member_copy(rel).start()
    for g in range(len(GROUPS)):
        mate_copy(g).wait_send()
        part_all(g).wait_send()
        row_all(g).wait_send()
        forward_copy(g).wait_send()
    every = pltpu.make_async_remote_copy(
        src_ref=got_ref, dst_ref=got_ref, send_sem=es_sem, recv_sem=er_sem, device_id=(m, to_m), device_id_type=MESH)
    every.wait_recv()
    total = moder
    for rel in range(1, MEMBERS):
        total += got_ref[rel - 1, 0:C, :]
    out_ref[0:C, :] = total * f32(1.0 / MEMBERS)
    out_ref[C:C + 1, :] = var
    every.wait_send()
    for cp in sends:
        cp.wait_send()


def laplace(hidden, proj, hw, hb, prior, labels, cw):
    vm = pl.BlockSpec(memory_space=pltpu.VMEM)
    any_ = pl.BlockSpec(memory_space=pl.ANY)
    dma = pltpu.SemaphoreType.DMA
    return pl.pallas_call(
        laplace_kernel,
        out_shape=jax.ShapeDtypeStruct((16, R_), f32),
        in_specs=[any_, any_, vm, vm, vm, vm, vm],
        out_specs=vm,
        scratch_shapes=[
            pltpu.VMEM((R_, 4096), bf16),
            pltpu.VMEM((8, 2 * KB, P_SIZE), bf16),
            pltpu.VMEM((R_, P_SIZE), f32),
            pltpu.VMEM((N, R_), bf16),
            pltpu.VMEM((N, R_), bf16),
            pltpu.VMEM((NB, B, N), f32),
            pltpu.VMEM((NB, B // 2, N), f32),
            pltpu.VMEM((NB, 56, N), f32),
            pltpu.VMEM((NB, B, N), f32),
            pltpu.VMEM((1, R_), f32),
            pltpu.VMEM((N + SLAB, W), f32),
            pltpu.VMEM((B, B), f32),
            pltpu.VMEM((N + SLAB, 3 * B), bf16),
            pltpu.VMEM((3 * B, W), bf16),
            pltpu.VMEM((16, R_), f32),
            pltpu.VMEM((MEMBERS - 1, 16, R_), f32),
            dma((2,)), dma((30,)), dma((16, 2)),
            dma((8,)), dma((8,)), dma((8,)), dma((8,)), dma((8,)), dma((8,)), dma((8,)), dma((8,)),
            dma, dma,
        ],
        compiler_params=pltpu.CompilerParams(
            collective_id=0, has_side_effects=True, vmem_limit_bytes=56 * 1024 * 1024),
    )(hidden, proj, hw, hb, prior, labels, cw)


def finish_kernel(pack_ref, var_ref, ens_ref):
    ens_ref[...] = pack_ref[0:C, :]
    var_ref[...] = pack_ref[C:C + 1, :]


def body(hidden, projection, head_weight, head_bias, prior_precision, labels, category_weight):
    pack = laplace(
        hidden[0], projection[0], head_weight[0], head_bias, prior_precision, labels[None, :], category_weight[None, :])
    vm = pl.BlockSpec(memory_space=pltpu.VMEM)
    return pl.pallas_call(
        finish_kernel,
        out_shape=(jax.ShapeDtypeStruct((1, R_), f32), jax.ShapeDtypeStruct((C, R_), f32)),
        in_specs=[vm],
        out_specs=(vm, vm),
    )(pack)


def solution(mesh):
    return jax.shard_map(
        body,
        mesh=mesh,
        in_specs=(
            P("member", "dp", None),
            P("member", "dp", None),
            P("member", None, None),
            P("member", None),
            P("member", None),
            P("dp"),
            P(),
        ),
        out_specs=(P("member", "dp"), P(None, "dp")),
        check_vma=False,
    )
```
